128 devices in a mesh: group: 8 (over y, core), local: 16 (over z, x).
Axes of the slice: x: 4, y: 4, z: 4, core: 2. Of those that a mesh axis runs over, the one named last changes fastest.
Arguments:
- lookup_grads: bfloat16 [1048576, 256], P(('group', 'local')), may hold values from -0.29882812 to 0.29882812
- slot_index: int32 [2, 1048576], P(None, ('group', 'local')), may hold values from 0 to 2047, as said below
- unique_rows: int32 [2, 16384], P(None, ('group', 'local')), may hold values from -1 to 131071, as said below
- tables: float32 [2, 131072, 256], P(None, ('group', 'local')), may hold values from -6 to 6
- accums: float32 [2, 131072], P(None, ('group', 'local')), may hold values from 0.01 to 1
Outputs:
- new_tables: float32 [2, 131072, 256], P(None, ('group', 'local'))
- new_accums: float32 [2, 131072], P(None, ('group', 'local'))
The draws below stay inside these ranges and needn't reach their ends.
Inputs may be any that keep to these rules, and one draw needn't show every extreme that they name: slot_index[t, i] names a slot of lookup i's group list whose entry in unique_rows[t] is not -1. `unique_rows`: table row p is owned by device p // 1024, which is device (group p // 16384, local p // 1024 % 16). Group g's list is entries g * 2048 to (g + 1) * 2048 - 1; its block l of 128 entries consists of 8 buckets of 16 entries, bucket h holding only rows owned by device (group h, local l), the used entries first and -1 after them. Rows within a group's list are distinct. In every draw and table some device (group h, local l) gets a full bucket from every group.
All inputs are finite; a program needn't handle non-finite values.
Results may differ from the reference program's by a relative error of at most 0.0003.
Values sent between devices are 32-bit elements; how exact they have to be, the bound alone decides.
No kernel may reach another device: no remote copies, remote signals or barrier semaphores. Data moves between devices by JAX's collectives and lax.ppermute only.
A program may use at most 64 MiB of HBM per device.

```python
import math
import jax
import jax.numpy as jnp
from jax import lax

EMB = 256
LOOK_DEV = 8192
CAP = 16
ROWS_DEV = 1024
SLOTS = 128
GROUP_SLOTS = 2048
ALL_SLOTS = 16384
LOOKUPS = 1048576
ROWS = 131072
N_GROUP = 8
N_LOCAL = 16


def shared_layout(key):
    base_key = jax.random.fold_in(key, 7)
    count_key, pick_key, offset_key, stride_key = jax.random.split(base_key, 4)
    bucket_shape = (2, N_GROUP, N_LOCAL, N_GROUP)
    live_count = jax.random.randint(count_key, bucket_shape, (CAP + 3) // 4, CAP + 1)
    local_pick = jax.random.randint(jax.random.fold_in(pick_key, 1), (2,), 0, N_LOCAL)
    group_pick = jax.random.randint(jax.random.fold_in(pick_key, 2), (2,), 0, N_GROUP)
    local_iota = jnp.arange(N_LOCAL)[None, None, :, None]
    group_iota = jnp.arange(N_GROUP)[None, None, None, :]
    marked = (local_iota == local_pick[:, None, None, None]) & (group_iota == group_pick[:, None, None, None])
    live_count = jnp.where(marked, CAP, live_count)
    return (live_count, offset_key, stride_key)


def draw_unique_rows(key, part):
    live_count, offset_key, stride_key = shared_layout(key)
    bucket_shape = (2, N_GROUP, N_LOCAL, N_GROUP)
    offset = jax.random.randint(offset_key, bucket_shape, 0, ROWS_DEV)
    stride = 2 * jax.random.randint(stride_key, bucket_shape, 0, max(ROWS_DEV // 2, 1)) + 1
    position = jnp.arange(CAP)
    local_rows = (offset[..., None] + stride[..., None] * position) % ROWS_DEV
    owners = jnp.arange(N_GROUP)[None, None, None, :] * N_LOCAL + jnp.arange(N_LOCAL)[None, None, :, None]
    row_ids = owners[..., None] * ROWS_DEV + local_rows
    row_ids = jnp.where(position < live_count[..., None], row_ids, -1)
    return row_ids.reshape(2, ALL_SLOTS).astype(jnp.int32)


def draw_slot_index(key, part):
    live_count, offset_key, stride_key = shared_layout(key)
    slot_key = jax.random.fold_in(key, 19)
    first_key, second_key, third_key = jax.random.split(slot_key, 3)
    local_choice = jax.random.randint(first_key, (2, LOOKUPS), 0, N_LOCAL)
    group_choice = jax.random.randint(second_key, (2, LOOKUPS), 0, N_GROUP)
    random_bits = jax.random.randint(third_key, (2, LOOKUPS), 0, 2 ** 20)
    group_of = jnp.arange(LOOKUPS) // (LOOK_DEV * N_LOCAL)
    table_of = jnp.arange(2)[:, None]
    available = live_count[table_of, group_of[None, :], local_choice, group_choice]
    slots = local_choice * SLOTS + group_choice * CAP + random_bits % available
    return slots.astype(jnp.int32)


def block_scale(key, shape, pieces, least, largest):
    factor_of, own = 1.0, jax.random.fold_in(key, 6)
    for axis_at, blocks in pieces:
        steps = jnp.exp(jax.random.uniform(jax.random.fold_in(own, axis_at), (blocks,), jnp.float32, least / len(pieces), largest / len(pieces)))
        factor_of = factor_of * jnp.repeat(steps, shape[axis_at] // blocks).reshape([-1 if axis == axis_at else 1 for axis in range(len(shape))])
    return factor_of


def noise(stream_key, extent, spread, bound, cuts=(), kind=jnp.bfloat16):
    result = spread * jax.random.normal(stream_key, extent, jnp.float32)
    if cuts:
        result = result * block_scale(stream_key, extent, cuts, -0.22, 0.18)
    return jnp.clip(result, -bound, bound).astype(kind)


def setup_inputs(seed: int = 0) -> dict:
    arg_keys = jax.random.split(jax.random.key(seed), 6)
    return {
        "lookup_grads": noise(arg_keys[0], (LOOKUPS, EMB), 0.05, 0.29882812, ((0, 128),)),
        "slot_index": draw_slot_index(jax.random.fold_in(arg_keys[5], 71), 0),
        "unique_rows": draw_unique_rows(jax.random.fold_in(arg_keys[5], 71), 0),
        "tables": noise(arg_keys[3], (2, ROWS, EMB), 1.0, 6.0, ((1, 128),), jnp.float32),
        "accums": jnp.clip(jnp.exp(math.log(1.0) - 4.6051702 * jax.random.uniform(arg_keys[4], (2, ROWS), jnp.float32) ** block_scale(arg_keys[4], (2, ROWS), ((1, 128),), -0.2, 0.2)), 0.01, 1.0),
    }


learning_rate = 0.1
epsilon = 1e-08

def reference(lookup_grads, slot_index, unique_rows, tables, accums):
    per_group = LOOK_DEV * N_LOCAL
    grouped = lookup_grads.reshape(N_GROUP, per_group, EMB)
    slots_grouped = jnp.transpose(slot_index.reshape(2, N_GROUP, per_group), (1, 0, 2))

    def group_total(inputs):
        gradients, slots_here = inputs
        wide = gradients.astype(jnp.float32)
        first = jax.ops.segment_sum(wide, slots_here[0], num_segments=GROUP_SLOTS)
        second = jax.ops.segment_sum(wide, slots_here[1], num_segments=GROUP_SLOTS)
        return jnp.stack([first, second])
    group_sums = lax.map(group_total, (grouped, slots_grouped))
    group_sums = jnp.transpose(group_sums, (1, 0, 2, 3)).reshape(2, ALL_SLOTS, EMB)
    new_tables = []
    new_accums = []
    for table_index in range(2):
        row_numbers = unique_rows[table_index]
        targets = jnp.where(row_numbers < 0, ROWS, row_numbers).astype(jnp.int32)
        row_grads = jnp.zeros((ROWS, EMB), jnp.float32).at[targets].add(group_sums[table_index], mode='drop')
        accum_new = accums[table_index] + lax.optimization_barrier(jnp.mean(row_grads * row_grads, axis=1))
        table_new = tables[table_index] - learning_rate * row_grads / (jnp.sqrt(accum_new)[:, None] + epsilon)
        new_tables.append(table_new)
        new_accums.append(accum_new)
    return (jnp.stack(new_tables), jnp.stack(new_accums))
```

```python
import jax
import jax.numpy as jnp
from jax import lax
from jax.experimental import pallas as pl
from jax.experimental.pallas import tpu as pltpu
from jax.sharding import PartitionSpec as P

learning_rate = 0.1
epsilon = 1e-08

AXES = ("group", "local")
SIDE = 4
CORES = 2
VMEM_BYTES = 40 << 20


def ring_pairs(n_group, n_local, stage, step):
    pairs = []
    for group in range(n_group):
        for place in range(n_local):
            z, x = divmod(place, SIDE)
            if (group % CORES + stage) % 2 == 0:
                x = (x + step) % SIDE
            else:
                z = (z + step) % SIDE
            pairs.append((group * n_local + place, group * n_local + z * SIDE + x))
    return pairs


def slot_sums(place, slot_index, lookup_grads, offsets):
    count, width = lookup_grads.shape
    slots = 128
    rows = SIDE * slots
    block = 1024

    def body(place_ref, index_ref, grads_ref, *out_refs):
        for start in range(0, count, block):
            grads = grads_ref[pl.ds(start, block), :]
            for table in range(2):
                index = index_ref[table : table + 1, pl.ds(start, block)]
                first = lax.shift_right_logical(index, place_ref[2]) & (SIDE - 1)
                second = lax.shift_right_logical(index, place_ref[3]) & (SIDE - 1)
                row = ((second - place_ref[1]) & (SIDE - 1)) * slots + (index & (slots - 1))
                mine = ((first - place_ref[0]) & (SIDE - 1)) == offsets[table]
                row = jnp.where(mine, row, -1)
                hit = lax.broadcasted_iota(jnp.int32, (rows, block), 0) == row
                onehot = jnp.where(hit, jnp.float32(1), jnp.float32(0)).astype(jnp.bfloat16)
                piece = jnp.dot(onehot, grads, preferred_element_type=jnp.float32)
                if start == 0:
                    out_refs[table][...] = piece
                else:
                    out_refs[table][...] += piece

    return pl.pallas_call(
        body,
        out_shape=[jax.ShapeDtypeStruct((rows, width), jnp.float32)] * 2,
        in_specs=[pl.BlockSpec(memory_space=pltpu.SMEM)]
        + [pl.BlockSpec(memory_space=pltpu.VMEM)] * 2,
        out_specs=[pl.BlockSpec(memory_space=pltpu.VMEM)] * 2,
        compiler_params=pltpu.CompilerParams(vmem_limit_bytes=VMEM_BYTES),
        cost_estimate=pl.CostEstimate(
            flops=4 * rows * count * width,
            bytes_accessed=count * width * 2 + rows * width * 8,
            transcendentals=0,
        ),
        name="slot_sums",
    )(place, slot_index, lookup_grads)


def apply_update(arrived, tables, accums):
    slots = arrived.shape[0]
    rows_dev, width = tables.shape[1:]
    parts = 2
    rows = rows_dev // parts
    lanes = 128

    def body(arrived_ref, tables_ref, accums_ref, new_tables_ref, new_accums_ref):
        half = pl.program_id(1)
        eye = lax.broadcasted_iota(jnp.int32, (lanes, lanes), 0) == lax.broadcasted_iota(
            jnp.int32, (lanes, lanes), 1
        )

        def update(table):
            values = arrived_ref[:, table * width : (table + 1) * width]
            high = values.astype(jnp.bfloat16)
            rest = values - high.astype(jnp.float32)
            middle = rest.astype(jnp.bfloat16)
            low = (rest - middle.astype(jnp.float32)).astype(jnp.bfloat16)
            pieces = jnp.concatenate([high, middle, low], axis=0)
            numbers = arrived_ref[:, 2 * width + table : 2 * width + table + 1]
            numbers = jnp.sum(
                jnp.where(eye, jnp.broadcast_to(numbers, (slots, lanes)), 0.0),
                axis=0,
                keepdims=True,
            ).astype(jnp.int32)
            hit = lax.broadcasted_iota(jnp.int32, (rows, slots), 0) + half * rows == numbers
            onehot = jnp.where(hit, jnp.float32(1), jnp.float32(0)).astype(jnp.bfloat16)
            onehot = jnp.concatenate([onehot] * 3, axis=1)
            row_grads = jnp.dot(onehot, pieces, preferred_element_type=jnp.float32)
            squares = jnp.sum(row_grads * row_grads, axis=1, keepdims=True)
            for start in range(0, rows, lanes):
                square = squares[start : start + lanes]
                square = jnp.sum(
                    jnp.where(eye, jnp.broadcast_to(square, (lanes, lanes)), 0.0),
                    axis=0,
                    keepdims=True,
                )
                accum = accums_ref[table : table + 1, pl.ds(half * rows + start, lanes)]
                accum = accum + square * (1.0 / width)
                new_accums_ref[table : table + 1, pl.ds(half * rows + start, lanes)] = accum
                scale = learning_rate / (jnp.sqrt(accum) + epsilon)
                scale = jnp.sum(
                    jnp.where(eye, jnp.broadcast_to(scale, (lanes, lanes)), 0.0),
                    axis=1,
                    keepdims=True,
                )
                new_tables_ref[0, start : start + lanes, :] = (
                    tables_ref[0, start : start + lanes, :]
                    - row_grads[start : start + lanes] * scale
                )

        for table in range(2):

            @pl.when(pl.program_id(0) == table)
            def _(table=table):
                update(table)

    return pl.pallas_call(
        body,
        grid=(2, parts),
        out_shape=[
            jax.ShapeDtypeStruct(tables.shape, jnp.float32),
            jax.ShapeDtypeStruct(accums.shape, jnp.float32),
        ],
        in_specs=[
            pl.BlockSpec(arrived.shape, lambda t, i: (0, 0)),
            pl.BlockSpec((1, rows, width), lambda t, i: (t, i, 0)),
            pl.BlockSpec(accums.shape, lambda t, i: (0, 0)),
        ],
        out_specs=[
            pl.BlockSpec((1, rows, width), lambda t, i: (t, i, 0)),
            pl.BlockSpec(accums.shape, lambda t, i: (0, 0)),
        ],
        compiler_params=pltpu.CompilerParams(vmem_limit_bytes=VMEM_BYTES),
        name="apply_update",
    )(arrived, tables, accums)


def local(lookup_grads, slot_index, unique_rows, tables, accums):
    n_group = lax.axis_size("group")
    n_local = lax.axis_size("local")
    rows_dev, width = tables.shape[1:]
    slots = unique_rows.shape[1]
    even = lax.axis_index("group") % CORES == 0
    z = lax.axis_index("local") // SIDE
    x = lax.axis_index("local") % SIDE
    place = jnp.stack(
        [
            jnp.where(even, x, z),
            jnp.where(even, z, x),
            jnp.where(even, 7, 9),
            jnp.where(even, 9, 7),
        ]
    ).astype(jnp.int32)

    def send(value, stage, step):
        return lax.ppermute(value, AXES, ring_pairs(n_group, n_local, stage, step))

    far0, far1 = slot_sums(place, slot_index, lookup_grads, (2, 2))
    far0 = send(far0, 0, 1)
    far1 = send(far1, 0, -1)
    back0, next1 = slot_sums(place, slot_index, lookup_grads, (3, 1))
    next1 = send(next1, 0, 1)
    back0 = send(back0, 0, -1)
    next0, back1 = slot_sums(place, slot_index, lookup_grads, (1, 3))
    next0 = send(next0 + far0, 0, 1)
    back1 = send(back1 + far1, 0, -1)
    own0, own1 = slot_sums(place, slot_index, lookup_grads, (0, 0))
    own0 = own0 + back0 + next0
    own1 = own1 + next1 + back1

    def part(value, offset):
        return value[offset * slots : (offset + 1) * slots]

    far0 = send(part(own0, 2), 1, 1)
    far1 = send(part(own1, 2), 1, -1)
    ahead = send(jnp.concatenate([part(own0, 1) + far0, part(own1, 1)]), 1, 1)
    behind = send(jnp.concatenate([part(own0, 3), part(own1, 3) + far1]), 1, -1)
    sum0 = part(own0, 0) + part(ahead, 0) + part(behind, 0)
    sum1 = part(own1, 0) + part(ahead, 1) + part(behind, 1)

    local_rows = jnp.where(unique_rows < 0, -1, unique_rows % rows_dev).astype(jnp.float32)
    local_rows = jnp.pad(jnp.transpose(local_rows), ((0, 0), (0, 126)))
    payload = jnp.concatenate([sum0, sum1, local_rows], axis=1)
    arrived = lax.all_to_all(payload, "group", split_axis=0, concat_axis=0, tiled=True)
    new_tables, new_accums = apply_update(arrived, tables, accums)
    return (new_tables, new_accums)


def solution(mesh):
    return jax.shard_map(
        local,
        mesh=mesh,
        in_specs=(
            P(("group", "local"), None),
            P(None, ("group", "local")),
            P(None, ("group", "local")),
            P(None, ("group", "local"), None),
            P(None, ("group", "local")),
        ),
        out_specs=(P(None, ("group", "local"), None), P(None, ("group", "local"))),
        check_vma=False,
    )
```

```python
import jax
import jax.numpy as jnp
from jax import lax
from jax.experimental import pallas as pl
from jax.experimental.pallas import tpu as pltpu
from jax.sharding import PartitionSpec as P

learning_rate = 0.1
epsilon = 1e-08

AXES = ("group", "local")
SIDE = 4
CORES = 2
LANES = 128
VMEM_BYTES = 16 << 20
FIRST_BYTES = 48 << 20
IN_VMEM = pl.BlockSpec(memory_space=pltpu.VMEM)
IN_SMEM = pl.BlockSpec(memory_space=pltpu.SMEM)
IN_HBM = pl.BlockSpec(memory_space=pltpu.HBM)


def ring_pairs(n_group, n_local, stage, step):
    pairs = []
    for group in range(n_group):
        for place in range(n_local):
            z, x = divmod(place, SIDE)
            if (group % CORES + stage) % 2 == 0:
                x = (x + step) % SIDE
            else:
                z = (z + step) % SIDE
            pairs.append((group * n_local + place, group * n_local + z * SIDE + x))
    return pairs


def call(body, name, out_shape, in_specs, out_specs=None, scratch=(), cost=None, vmem=VMEM_BYTES):
    return pl.pallas_call(
        body,
        out_shape=out_shape,
        in_specs=in_specs,
        out_specs=[IN_VMEM] * len(out_shape) if out_specs is None else out_specs,
        scratch_shapes=scratch,
        compiler_params=pltpu.CompilerParams(vmem_limit_bytes=vmem),
        cost_estimate=cost,
        name=name,
    )


def f32(*shape):
    return jax.ShapeDtypeStruct(shape, jnp.float32)


def kernel_cost(rows, count, width):
    return pl.CostEstimate(
        flops=4 * rows * count * width // 10, bytes_accessed=count * width // 5, transcendentals=0
    )


def add_block(codes, grads, offsets, start, out_refs):
    rows = out_refs[0].shape[0]
    for table in range(2):
        target = lax.broadcasted_iota(jnp.int32, (rows, grads.shape[0]), 0) + offsets[table] * rows
        hit = target == codes[table : table + 1]
        onehot = jnp.where(hit, jnp.float32(1), jnp.float32(0)).astype(jnp.bfloat16)
        piece = jnp.dot(onehot, grads, preferred_element_type=jnp.float32)
        if start == 0:
            out_refs[table][...] = piece
        else:
            out_refs[table][...] += piece


def first_sums(place, slot_index, lookup_grads, offsets):
    count, width = lookup_grads.shape
    rows = SIDE * LANES
    block = 1024
    blocks = count // block

    def body(place_ref, index_hbm, grads_hbm, out0, out1, grads_ref, codes_ref, index_ref, sems):
        copies = [pltpu.make_async_copy(index_hbm, index_ref, sems.at[blocks])]
        for i in range(blocks):
            piece = pl.ds(i * block, block)
            copies.append(
                pltpu.make_async_copy(grads_hbm.at[piece], grads_ref.at[piece], sems.at[i])
            )
        for copy in copies:
            copy.start()
        copies[0].wait()
        index = index_ref[...]
        first = lax.shift_right_logical(index, place_ref[2]) & (SIDE - 1)
        second = lax.shift_right_logical(index, place_ref[3]) & (SIDE - 1)
        first = (first - place_ref[0]) & (SIDE - 1)
        second = (second - place_ref[1]) & (SIDE - 1)
        codes_ref[...] = first * rows + second * LANES + (index & (LANES - 1))
        for i in range(blocks):
            copies[1 + i].wait()
            piece = pl.ds(i * block, block)
            add_block(codes_ref[:, piece], grads_ref[piece, :], offsets, i, (out0, out1))

    return call(
        body,
        "first_sums",
        [
            f32(rows, width),
            f32(rows, width),
            jax.ShapeDtypeStruct(lookup_grads.shape, lookup_grads.dtype),
            jax.ShapeDtypeStruct(slot_index.shape, jnp.int32),
        ],
        [IN_SMEM, IN_HBM, IN_HBM],
        scratch=[
            pltpu.VMEM(slot_index.shape, jnp.int32),
            pltpu.SemaphoreType.DMA((blocks + 1,)),
        ],
        cost=kernel_cost(rows, count, width),
        vmem=FIRST_BYTES,
    )(place, slot_index, lookup_grads)


def slot_sums(codes, lookup_grads, offsets):
    count, width = lookup_grads.shape
    rows = SIDE * LANES
    block = 1024

    def body(codes_ref, grads_ref, out0, out1):
        for start in range(0, count, block):
            piece = pl.ds(start, block)
            add_block(codes_ref[:, piece], grads_ref[piece, :], offsets, start, (out0, out1))

    return call(
        body,
        "slot_sums",
        [f32(rows, width)] * 2,
        [IN_VMEM] * 2,
        cost=kernel_cost(rows, count, width),
    )(codes, lookup_grads)


def finish_first_ring(own0, back0, next0, own1, next1, back1):
    slots, width = LANES, own0.shape[1]

    def body(o0, b0, n0, o1, n1, b1, far0, far1, ahead, behind, own):
        def total(table, offset):
            piece = pl.ds(offset * slots, slots)
            refs = (o0, b0, n0) if table == 0 else (o1, n1, b1)
            return refs[0][piece, :] + refs[1][piece, :] + refs[2][piece, :]

        far0[...] = total(0, 2)
        far1[...] = total(1, 2)
        for table in range(2):
            piece = pl.ds(table * slots, slots)
            ahead[piece, :] = total(table, 1)
            behind[piece, :] = total(table, 3)
            own[piece, :] = total(table, 0)

    return call(
        body,
        "finish_first_ring",
        [f32(slots, width)] * 2 + [f32(2 * slots, width)] * 3,
        [IN_VMEM] * 6,
    )(own0, back0, next0, own1, next1, back1)


def add_far(ahead, far0, behind, far1):
    slots = LANES

    def body(a, f0, b, f1, new_a, new_b):
        low, high = pl.ds(0, slots), pl.ds(slots, slots)
        new_a[low, :] = a[low, :] + f0[...]
        new_a[high, :] = a[high, :]
        new_b[low, :] = b[low, :]
        new_b[high, :] = b[high, :] + f1[...]

    return call(body, "add_far", [f32(*ahead.shape)] * 2, [IN_VMEM] * 4)(ahead, far0, behind, far1)


def eye():
    shape = (LANES, LANES)
    return lax.broadcasted_iota(jnp.int32, shape, 0) == lax.broadcasted_iota(jnp.int32, shape, 1)


def turn(vector, diagonal):
    axis = 1 if vector.shape[0] == 1 else 0
    square = jnp.where(diagonal, jnp.broadcast_to(vector, (LANES, LANES)), 0.0)
    return jnp.sum(square, axis=axis, keepdims=True)


def finish_second_ring(own, ahead, behind, unique_rows, rows_dev):
    slots, width = LANES, own.shape[1]

    def body(o, a, b, unique_ref, payload):
        diagonal = eye()
        for table in range(2):
            piece = pl.ds(table * slots, slots)
            payload[:, pl.ds(table * width, width)] = o[piece, :] + a[piece, :] + b[piece, :]
            numbers = unique_ref[table : table + 1, :]
            numbers = jnp.where(numbers < 0, -1, numbers & (rows_dev - 1)).astype(jnp.float32)
            column = pl.ds((2 * width) + table * LANES, LANES)
            payload[:, column] = jnp.broadcast_to(turn(numbers, diagonal), (slots, LANES))

    return call(body, "finish_second_ring", [f32(slots, 2 * width + 2 * LANES)], [IN_VMEM] * 4)(
        own, ahead, behind, unique_rows
    )[0]


def apply_update(arrived, tables, accums):
    rows_dev, width = tables.shape[1:]
    rows = 256
    count = rows_dev // rows

    def body(arrived_ref, tables_ref, accums_ref, new_tables_hbm, new_accums_ref, done_ref, sems):
        diagonal = eye()
        copies = []
        for table in range(2):
            values = arrived_ref[:, table * width : (table + 1) * width]
            high = values.astype(jnp.bfloat16)
            rest = values - high.astype(jnp.float32)
            middle = rest.astype(jnp.bfloat16)
            low = (rest - middle.astype(jnp.float32)).astype(jnp.bfloat16)
            pieces = jnp.concatenate([high, middle, low], axis=0)
            first = 2 * width + table * LANES
            numbers = jnp.where(diagonal, arrived_ref[:, first : first + LANES], 0.0)
            numbers = jnp.sum(numbers, axis=0, keepdims=True).astype(jnp.int32)
            for block in range(count):
                base = block * rows
                hit = lax.broadcasted_iota(jnp.int32, (rows, LANES), 0) + base == numbers
                onehot = jnp.where(hit, jnp.float32(1), jnp.float32(0)).astype(jnp.bfloat16)
                onehot = jnp.concatenate([onehot] * 3, axis=1)
                row_grads = jnp.dot(onehot, pieces, preferred_element_type=jnp.float32)
                squares = jnp.sum(row_grads * row_grads, axis=1, keepdims=True)
                for start in range(0, rows, LANES):
                    place = pl.ds(base + start, LANES)
                    square = turn(squares[start : start + LANES], diagonal)
                    accum = accums_ref[table : table + 1, place] + square * (1.0 / width)
                    new_accums_ref[table : table + 1, place] = accum
                    scale = turn(learning_rate / (jnp.sqrt(accum) + epsilon), diagonal)
                    step = row_grads[start : start + LANES] * scale
                    done_ref[table, place, :] = tables_ref[table, place, :] - step
                place = pl.ds(base, rows)
                copies.append(
                    pltpu.make_async_copy(
                        done_ref.at[table, place],
                        new_tables_hbm.at[table, place],
                        sems.at[table * count + block],
                    )
                )
                copies[-1].start()
        for copy in copies:
            copy.wait()

    return call(
        body,
        "apply_update",
        [f32(*tables.shape), f32(*accums.shape)],
        [IN_VMEM] * 3,
        [IN_HBM, IN_VMEM],
        [pltpu.VMEM(tables.shape, jnp.float32), pltpu.SemaphoreType.DMA((2 * count,))],
    )(arrived, tables, accums)


def local(lookup_grads, slot_index, unique_rows, tables, accums):
    n_group = lax.axis_size("group")
    n_local = lax.axis_size("local")
    even = lax.axis_index("group") & 1 == 0
    z = lax.shift_right_logical(lax.axis_index("local"), 2)
    x = lax.axis_index("local") & (SIDE - 1)
    place = jnp.stack(
        [
            jnp.where(even, x, z),
            jnp.where(even, z, x),
            jnp.where(even, 7, 9),
            jnp.where(even, 9, 7),
        ]
    ).astype(jnp.int32)

    def send(value, stage, step):
        return lax.ppermute(value, AXES, ring_pairs(n_group, n_local, stage, step))

    far0, far1, grads, codes = first_sums(place, slot_index, lookup_grads, (2, 2))
    far0 = send(far0, 0, 1)
    far1 = send(far1, 0, -1)
    back0, next1 = slot_sums(codes, grads, (3, 1))
    next1 = send(next1, 0, 1)
    back0 = send(back0, 0, -1)
    next0, back1 = slot_sums(codes, grads, (1, 3))
    next0 = send(next0 + far0, 0, 1)
    back1 = send(back1 + far1, 0, -1)
    own0, own1 = slot_sums(codes, grads, (0, 0))

    far0, far1, ahead, behind, own = finish_first_ring(own0, back0, next0, own1, next1, back1)
    far0 = send(far0, 1, 1)
    far1 = send(far1, 1, -1)
    ahead, behind = add_far(ahead, far0, behind, far1)
    ahead = send(ahead, 1, 1)
    behind = send(behind, 1, -1)
    payload = finish_second_ring(own, ahead, behind, unique_rows, tables.shape[1])

    arrived = lax.all_to_all(payload, "group", split_axis=0, concat_axis=0, tiled=True)
    new_tables, new_accums = apply_update(arrived, tables, accums)
    return (new_tables, new_accums)


def solution(mesh):
    return jax.shard_map(
        local,
        mesh=mesh,
        in_specs=(
            P(("group", "local"), None),
            P(None, ("group", "local")),
            P(None, ("group", "local")),
            P(None, ("group", "local"), None),
            P(None, ("group", "local")),
        ),
        out_specs=(P(None, ("group", "local"), None), P(None, ("group", "local"))),
        check_vma=False,
    )
```

```python
import jax
import jax.numpy as jnp
from jax import lax
from jax.experimental import pallas as pl
from jax.experimental.pallas import tpu as pltpu
from jax.sharding import PartitionSpec as P

learning_rate = 0.1
epsilon = 1e-08

AXES = ("group", "local")
SIDE = 4
CORES = 2
LANES = 128
VMEM_BYTES = 16 << 20
FIRST_BYTES = 48 << 20
IN_VMEM = pl.BlockSpec(memory_space=pltpu.VMEM)
IN_SMEM = pl.BlockSpec(memory_space=pltpu.SMEM)
IN_HBM = pl.BlockSpec(memory_space=pltpu.HBM)


def ring_pairs(n_group, n_local, step):
    pairs = []
    for group in range(n_group):
        for place in range(n_local):
            z, x = divmod(place, SIDE)
            if group % CORES == 0:
                x = (x + step) % SIDE
            else:
                z = (z + step) % SIDE
            pairs.append((group * n_local + place, group * n_local + z * SIDE + x))
    return pairs


def second_groups(n_group, n_local):
    groups = []
    for core in range(CORES):
        for first in range(SIDE):
            members = []
            for chip in range(n_group // CORES):
                for second in range(SIDE):
                    z, x = (second, first) if core == 0 else (first, second)
                    members.append((chip * CORES + core) * n_local + z * SIDE + x)
            groups.append(members)
    return groups


def call(body, name, out_shape, in_specs, out_specs=None, scratch=(), cost=None, vmem=VMEM_BYTES):
    return pl.pallas_call(
        body,
        out_shape=out_shape,
        in_specs=in_specs,
        out_specs=[IN_VMEM] * len(out_shape) if out_specs is None else out_specs,
        scratch_shapes=scratch,
        compiler_params=pltpu.CompilerParams(vmem_limit_bytes=vmem),
        cost_estimate=cost,
        name=name,
    )


def f32(*shape):
    return jax.ShapeDtypeStruct(shape, jnp.float32)


def kernel_cost(rows, count, width):
    return pl.CostEstimate(
        flops=4 * rows * count * width // 10, bytes_accessed=count * width // 5, transcendentals=0
    )


def add_block(codes, grads, targets, start, out_refs):
    rows = out_refs[0].shape[0]
    for (table, offset), out_ref in zip(targets, out_refs):
        target = lax.broadcasted_iota(jnp.int32, (rows, grads.shape[0]), 0) + offset * rows
        hit = target == codes[table : table + 1]
        onehot = jnp.where(hit, jnp.float32(1), jnp.float32(0)).astype(jnp.bfloat16)
        piece = jnp.dot(onehot, grads, preferred_element_type=jnp.float32)
        if start == 0:
            out_ref[...] = piece
        else:
            out_ref[...] += piece


def first_sums(place, slot_index, lookup_grads, targets):
    count, width = lookup_grads.shape
    rows = SIDE * LANES
    block = 1024
    blocks = count // block

    def body(place_ref, index_ref, grads_hbm, *refs):
        out_refs = refs[: len(targets)]
        grads_ref, codes_ref, sems = refs[len(targets) :]
        copies = []
        for i in range(blocks):
            piece = pl.ds(i * block, block)
            copies.append(
                pltpu.make_async_copy(grads_hbm.at[piece], grads_ref.at[piece], sems.at[i])
            )
        for copy in copies:
            copy.start()
        index = index_ref[...]
        first = lax.shift_right_logical(index, place_ref[2]) & (SIDE - 1)
        second = lax.shift_right_logical(index, place_ref[3]) & (SIDE - 1)
        first = (first - place_ref[0]) & (SIDE - 1)
        codes_ref[...] = first * rows + second * LANES + (index & (LANES - 1))
        for i in range(blocks):
            copies[i].wait()
            piece = pl.ds(i * block, block)
            add_block(codes_ref[:, piece], grads_ref[piece, :], targets, i, out_refs)

    return call(
        body,
        "first_sums",
        [
            *[f32(rows, width) for _ in targets],
            jax.ShapeDtypeStruct(lookup_grads.shape, lookup_grads.dtype),
            jax.ShapeDtypeStruct(slot_index.shape, jnp.int32),
        ],
        [IN_SMEM, IN_VMEM, IN_HBM],
        scratch=[
            pltpu.SemaphoreType.DMA((blocks,)),
        ],
        cost=kernel_cost(rows, count, width),
        vmem=FIRST_BYTES,
    )(place, slot_index, lookup_grads)


def slot_sums(codes, lookup_grads, targets):
    count, width = lookup_grads.shape
    rows = SIDE * LANES
    block = 1024

    def body(codes_ref, grads_ref, *out_refs):
        for start in range(0, count, block):
            piece = pl.ds(start, block)
            add_block(codes_ref[:, piece], grads_ref[piece, :], targets, start, out_refs)

    return call(
        body,
        "slot_sums",
        [f32(rows, width) for _ in targets],
        [IN_VMEM] * 2,
        cost=kernel_cost(rows, count, width),
    )(codes, lookup_grads)


def finish_first_ring(place, unique_rows, own0, back0, next0, own1, next1, back1):
    rows, width = own0.shape
    chips = SIDE
    block = rows // SIDE // chips
    tiles = 2 * width // LANES

    def body(place_ref, unique_ref, o0, b0, n0, o1, n1, b1, spread):
        numbers = unique_ref[...].astype(jnp.float32) + 1.0
        numbers = jnp.concatenate([numbers, jnp.zeros((6, LANES), jnp.float32)], axis=0)
        for second in range(SIDE):
            mine = jnp.where(place_ref[1] == second, numbers, 0.0)
            for chip in range(chips):
                member = chip * SIDE + second
                piece = pl.ds((second * chips + chip) * block, block)
                for table, refs in enumerate([(o0, b0, n0), (o1, n1, b1)]):
                    total = refs[0][piece, :] + refs[1][piece, :] + refs[2][piece, :]
                    for tile in range(tiles // 2):
                        spot = pl.ds((table * (tiles // 2) + tile) * block, block)
                        spread[member, spot, :] = total[:, tile * LANES : (tile + 1) * LANES]
                spread[member, pl.ds(tiles * block, 8), :] = mine

    return call(
        body,
        "finish_first_ring",
        [f32(SIDE * chips, tiles * block + 8, LANES)],
        [IN_SMEM] + [IN_VMEM] * 7,
    )(place, unique_rows, own0, back0, next0, own1, next1, back1)[0]


def finish_second_ring(place, spread):
    members, rows, lanes = spread.shape
    chips = members // SIDE
    half = LANES // 8
    tiles = (rows - 8) // (CORES * half)

    def body(place_ref, spread_ref, kept, given):
        core = place_ref[4] & 1

        def total(chip, piece):
            pieces = [spread_ref[chip * SIDE + second, piece, :] for second in range(SIDE)]
            return (pieces[0] + pieces[1]) + (pieces[2] + pieces[3])

        for chip in range(chips):
            for tile in range(tiles):
                low = total(chip, pl.ds(tile * CORES * half, half))
                high = total(chip, pl.ds(tile * CORES * half + half, half))
                spot = pl.ds(tile * half, half)
                kept[chip, spot, :] = jnp.where(core == 0, low, high)
                given[chip, spot, :] = jnp.where(core == 0, high, low)
            numbers = total(chip, pl.ds(rows - 8, 8))
            kept[chip, pl.ds(tiles * half, 8), :] = numbers
            given[chip, pl.ds(tiles * half, 8), :] = numbers

    return call(
        body, "finish_second_ring", [f32(chips, tiles * half + 8, lanes)] * 2, [IN_SMEM, IN_VMEM]
    )(place, spread)


def eye():
    shape = (LANES, LANES)
    return lax.broadcasted_iota(jnp.int32, shape, 0) == lax.broadcasted_iota(jnp.int32, shape, 1)


def turn(vector, diagonal):
    axis = 1 if vector.shape[0] == 1 else 0
    square = jnp.where(diagonal, jnp.broadcast_to(vector, (LANES, LANES)), 0.0)
    return jnp.sum(square, axis=axis, keepdims=True)


def apply_update(place, kept, swapped, tables, accums):
    rows_dev, width = tables.shape[1:]
    rows = 256
    count = rows_dev // rows

    chips, slots = kept.shape[:2]
    bucket = LANES // (CORES * chips)
    slots -= 8
    tiles = width // LANES

    def body(place_ref, kept_ref, swapped_ref, tables_ref, accums_ref, *refs):
        new_tables_hbm, new_accums_ref, done_ref, sems = refs
        diagonal = eye()
        copies = []
        sources = [(ref, chip) for ref in (kept_ref, swapped_ref) for chip in range(chips)]
        group = place_ref[4]
        lane = lax.broadcasted_iota(jnp.int32, (8, LANES), 1) // bucket
        local_rows = jnp.zeros((8, LANES), jnp.int32)
        for spot, (ref, chip) in enumerate(sources):
            listed = ref[chip, pl.ds(slots, 8), :].astype(jnp.int32)
            listed = pltpu.roll(listed, ((spot - group) * bucket) & (LANES - 1), 1)
            local_rows = jnp.where(lane == spot, listed, local_rows)
        local_rows = jnp.where(local_rows == 0, -1, (local_rows - 1) & (rows_dev - 1))
        for table in range(2):
            columns = []
            for tile in range(table * tiles, (table + 1) * tiles):
                spot = pl.ds(tile * bucket, bucket)
                columns.append(jnp.concatenate([ref[chip, spot, :] for ref, chip in sources]))
            values = jnp.concatenate(columns, axis=1)
            high = values.astype(jnp.bfloat16)
            rest = values - high.astype(jnp.float32)
            middle = rest.astype(jnp.bfloat16)
            low = (rest - middle.astype(jnp.float32)).astype(jnp.bfloat16)
            pieces = jnp.concatenate([high, middle, low], axis=0)
            for block in range(count):
                base = block * rows
                hit = lax.broadcasted_iota(jnp.int32, (rows, LANES), 0) + base == local_rows[table : table + 1]
                onehot = jnp.where(hit, jnp.float32(1), jnp.float32(0)).astype(jnp.bfloat16)
                onehot = jnp.concatenate([onehot] * 3, axis=1)
                row_grads = jnp.dot(onehot, pieces, preferred_element_type=jnp.float32)
                squares = jnp.sum(row_grads * row_grads, axis=1, keepdims=True)
                for start in range(0, rows, LANES):
                    place = pl.ds(base + start, LANES)
                    square = turn(squares[start : start + LANES], diagonal)
                    accum = accums_ref[table : table + 1, place] + square * (1.0 / width)
                    new_accums_ref[table : table + 1, place] = accum
                    scale = turn(learning_rate / (jnp.sqrt(accum) + epsilon), diagonal)
                    step = row_grads[start : start + LANES] * scale
                    done_ref[table, place, :] = tables_ref[table, place, :] - step
                place = pl.ds(base, rows)
                copies.append(
                    pltpu.make_async_copy(
                        done_ref.at[table, place],
                        new_tables_hbm.at[table, place],
                        sems.at[table * count + block],
                    )
                )
                copies[-1].start()
        for copy in copies:
            copy.wait()

    return call(
        body,
        "apply_update",
        [f32(*tables.shape), f32(*accums.shape)],
        [IN_SMEM] + [IN_VMEM] * 4,
        [IN_HBM, IN_VMEM],
        [pltpu.VMEM(tables.shape, jnp.float32), pltpu.SemaphoreType.DMA((2 * count,))],
    )(place, kept, swapped, tables, accums)


def local(lookup_grads, slot_index, unique_rows, tables, accums):
    n_group = lax.axis_size("group")
    n_local = lax.axis_size("local")
    even = lax.axis_index("group") & 1 == 0
    z = lax.shift_right_logical(lax.axis_index("local"), 2)
    x = lax.axis_index("local") & (SIDE - 1)
    place = jnp.stack(
        [
            jnp.where(even, x, z),
            jnp.where(even, z, x),
            jnp.where(even, 7, 9),
            jnp.where(even, 9, 7),
            lax.axis_index("group"),
        ]
    ).astype(jnp.int32)

    def send(value, step):
        return lax.ppermute(value, AXES, ring_pairs(n_group, n_local, step))

    far0, far1, grads, codes = first_sums(place, slot_index, lookup_grads, [(0, 2), (1, 2)])
    far0 = send(far0, 1)
    far1 = send(far1, -1)
    back0, next1 = slot_sums(codes, grads, [(0, 3), (1, 1)])
    next1 = send(next1, 1)
    back0 = send(back0, -1)
    next0, back1 = slot_sums(codes, grads, [(0, 1), (1, 3)])
    next0 = send(next0 + far0, 1)
    back1 = send(back1 + far1, -1)
    own0, own1 = slot_sums(codes, grads, [(0, 0), (1, 0)])

    spread = finish_first_ring(place, unique_rows, own0, back0, next0, own1, next1, back1)
    spread = lax.all_to_all(
        spread,
        AXES,
        split_axis=0,
        concat_axis=0,
        axis_index_groups=second_groups(n_group, n_local),
        tiled=True,
    )
    kept, given = finish_second_ring(place, spread)

    swapped = lax.ppermute(given, "group", [(i, i ^ 1) for i in range(n_group)])
    new_tables, new_accums = apply_update(place, kept, swapped, tables, accums)
    return (new_tables, new_accums)


def solution(mesh):
    return jax.shard_map(
        local,
        mesh=mesh,
        in_specs=(
            P(("group", "local"), None),
            P(None, ("group", "local")),
            P(None, ("group", "local")),
            P(None, ("group", "local"), None),
            P(None, ("group", "local")),
        ),
        out_specs=(P(None, ("group", "local"), None), P(None, ("group", "local"))),
        check_vma=False,
    )
```

```python
import jax
import jax.numpy as jnp
from jax import lax
from jax.experimental import pallas as pl
from jax.experimental.pallas import tpu as pltpu
from jax.sharding import PartitionSpec as P

learning_rate = 0.1
epsilon = 1e-08

AXES = ("group", "local")
SIDE = 4
CORES = 2
LANES = 128
VMEM_BYTES = 16 << 20
FIRST_BYTES = 48 << 20
IN_VMEM = pl.BlockSpec(memory_space=pltpu.VMEM)
IN_HBM = pl.BlockSpec(memory_space=pltpu.HBM)


def ring_pairs(n_group, n_local, step):
    pairs = []
    for group in range(n_group):
        for place in range(n_local):
            z, x = divmod(place, SIDE)
            if group % CORES == 0:
                x = (x + step) % SIDE
            else:
                z = (z + step) % SIDE
            pairs.append((group * n_local + place, group * n_local + z * SIDE + x))
    return pairs


def position():
    group = lax.axis_index("group")
    place = lax.axis_index("local")
    z, x = lax.shift_right_logical(place, 2), place & (SIDE - 1)
    even = group & (CORES - 1) == 0
    return group, jnp.where(even, x, z), jnp.where(even, z, x), even


def second_groups(n_group, n_local):
    groups = []
    for core in range(CORES):
        for first in range(SIDE):
            members = []
            for chip in range(n_group // CORES):
                for second in range(SIDE):
                    z, x = (second, first) if core == 0 else (first, second)
                    members.append((chip * CORES + core) * n_local + z * SIDE + x)
            groups.append(members)
    return groups


def call(body, name, out_shape, in_specs, out_specs=None, scratch=(), cost=None, vmem=VMEM_BYTES):
    return pl.pallas_call(
        body,
        out_shape=out_shape,
        in_specs=in_specs,
        out_specs=[IN_VMEM] * len(out_shape) if out_specs is None else out_specs,
        scratch_shapes=scratch,
        compiler_params=pltpu.CompilerParams(vmem_limit_bytes=vmem),
        cost_estimate=cost,
        name=name,
    )


def f32(*shape):
    return jax.ShapeDtypeStruct(shape, jnp.float32)


def kernel_cost(rows, count, width):
    return pl.CostEstimate(
        flops=4 * rows * count * width // 10, bytes_accessed=count * width // 5, transcendentals=0
    )


def add_block(codes, grads, targets, start, out_refs):
    rows = out_refs[0].shape[0]
    for (table, offset), out_ref in zip(targets, out_refs):
        target = lax.broadcasted_iota(jnp.int32, (rows, grads.shape[0]), 0) + offset * rows
        hit = target == codes[table : table + 1]
        onehot = jnp.where(hit, jnp.float32(1), jnp.float32(0)).astype(jnp.bfloat16)
        piece = jnp.dot(onehot, grads, preferred_element_type=jnp.float32)
        if start == 0:
            out_ref[...] = piece
        else:
            out_ref[...] += piece


def first_sums(slot_index, lookup_grads, targets):
    count, width = lookup_grads.shape
    rows = SIDE * LANES
    block = 1024
    blocks = count // block

    def body(index_ref, grads_hbm, *refs):
        out_refs = refs[: len(targets)]
        grads_ref, codes_ref, sems = refs[len(targets) :]
        copies = []
        for i in range(blocks):
            piece = pl.ds(i * block, block)
            copies.append(
                pltpu.make_async_copy(grads_hbm.at[piece], grads_ref.at[piece], sems.at[i])
            )
        for copy in copies:
            copy.start()
        _, own_first, _, even = position()
        index = index_ref[...]
        first = lax.shift_right_logical(index, jnp.where(even, 7, 9)) & (SIDE - 1)
        second = lax.shift_right_logical(index, jnp.where(even, 9, 7)) & (SIDE - 1)
        first = (first - own_first) & (SIDE - 1)
        codes_ref[...] = first * rows + second * LANES + (index & (LANES - 1))
        for i in range(blocks):
            copies[i].wait()
            piece = pl.ds(i * block, block)
            add_block(codes_ref[:, piece], grads_ref[piece, :], targets, i, out_refs)

    return call(
        body,
        "first_sums",
        [
            *[f32(rows, width) for _ in targets],
            jax.ShapeDtypeStruct(lookup_grads.shape, lookup_grads.dtype),
            jax.ShapeDtypeStruct(slot_index.shape, jnp.int32),
        ],
        [IN_VMEM, IN_HBM],
        scratch=[
            pltpu.SemaphoreType.DMA((blocks,)),
        ],
        cost=kernel_cost(rows, count, width),
        vmem=FIRST_BYTES,
    )(slot_index, lookup_grads)


def slot_sums(codes, lookup_grads, targets):
    count, width = lookup_grads.shape
    rows = SIDE * LANES
    block = 1024

    def body(codes_ref, grads_ref, *out_refs):
        for start in range(0, count, block):
            piece = pl.ds(start, block)
            add_block(codes_ref[:, piece], grads_ref[piece, :], targets, start, out_refs)

    return call(
        body,
        "slot_sums",
        [f32(rows, width) for _ in targets],
        [IN_VMEM] * 2,
        cost=kernel_cost(rows, count, width),
    )(codes, lookup_grads)


def finish_first_ring(unique_rows, own0, back0, next0, own1, next1, back1):
    rows, width = own0.shape
    chips = SIDE
    block = rows // SIDE // chips
    tiles = 2 * width // LANES

    def body(unique_ref, o0, b0, n0, o1, n1, b1, spread):
        own_second = position()[2]
        numbers = unique_ref[...].astype(jnp.float32) + 1.0
        numbers = jnp.concatenate([numbers, jnp.zeros((6, LANES), jnp.float32)], axis=0)
        for second in range(SIDE):
            mine = jnp.where(own_second == second, numbers, 0.0)
            for chip in range(chips):
                member = chip * SIDE + second
                piece = pl.ds((second * chips + chip) * block, block)
                for table, refs in enumerate([(o0, b0, n0), (o1, n1, b1)]):
                    total = refs[0][piece, :] + refs[1][piece, :] + refs[2][piece, :]
                    for tile in range(tiles // 2):
                        spot = pl.ds((table * (tiles // 2) + tile) * block, block)
                        spread[member, spot, :] = total[:, tile * LANES : (tile + 1) * LANES]
                spread[member, pl.ds(tiles * block, 8), :] = mine

    return call(
        body,
        "finish_first_ring",
        [f32(SIDE * chips, tiles * block + 8, LANES)],
        [IN_VMEM] * 7,
    )(unique_rows, own0, back0, next0, own1, next1, back1)[0]


def finish_second_ring(spread):
    members, rows, lanes = spread.shape
    chips = members // SIDE
    half = LANES // 8
    tiles = (rows - 8) // (CORES * half)

    def body(spread_ref, kept, given):
        even = position()[3]

        def total(chip, piece):
            pieces = [spread_ref[chip * SIDE + second, piece, :] for second in range(SIDE)]
            return (pieces[0] + pieces[1]) + (pieces[2] + pieces[3])

        for chip in range(chips):
            for tile in range(tiles):
                low = total(chip, pl.ds(tile * CORES * half, half))
                high = total(chip, pl.ds(tile * CORES * half + half, half))
                spot = pl.ds(tile * half, half)
                kept[chip, spot, :] = jnp.where(even, low, high)
                given[chip, spot, :] = jnp.where(even, high, low)
            numbers = total(chip, pl.ds(rows - 8, 8))
            kept[chip, pl.ds(tiles * half, 8), :] = numbers
            given[chip, pl.ds(tiles * half, 8), :] = numbers

    return call(
        body, "finish_second_ring", [f32(chips, tiles * half + 8, lanes)] * 2, [IN_VMEM]
    )(spread)


def eye():
    shape = (LANES, LANES)
    return lax.broadcasted_iota(jnp.int32, shape, 0) == lax.broadcasted_iota(jnp.int32, shape, 1)


def turn(vector, diagonal):
    axis = 1 if vector.shape[0] == 1 else 0
    square = jnp.where(diagonal, jnp.broadcast_to(vector, (LANES, LANES)), 0.0)
    return jnp.sum(square, axis=axis, keepdims=True)


def apply_update(kept, swapped, tables, accums):
    rows_dev, width = tables.shape[1:]
    rows = 256
    count = rows_dev // rows

    chips, slots = kept.shape[:2]
    bucket = LANES // (CORES * chips)
    slots -= 8
    tiles = width // LANES

    def body(kept_ref, swapped_ref, tables_ref, accums_ref, *refs):
        new_tables_hbm, new_accums_ref, done_ref, sems = refs
        diagonal = eye()
        copies = []
        sources = [(ref, chip) for ref in (kept_ref, swapped_ref) for chip in range(chips)]
        group = position()[0]
        lane = lax.broadcasted_iota(jnp.int32, (8, LANES), 1) // bucket
        local_rows = jnp.zeros((8, LANES), jnp.int32)
        for spot, (ref, chip) in enumerate(sources):
            listed = ref[chip, pl.ds(slots, 8), :].astype(jnp.int32)
            listed = pltpu.roll(listed, ((spot - group) * bucket) & (LANES - 1), 1)
            local_rows = jnp.where(lane == spot, listed, local_rows)
        local_rows = jnp.where(local_rows == 0, -1, (local_rows - 1) & (rows_dev - 1))
        for table in range(2):
            columns = []
            for tile in range(table * tiles, (table + 1) * tiles):
                spot = pl.ds(tile * bucket, bucket)
                columns.append(jnp.concatenate([ref[chip, spot, :] for ref, chip in sources]))
            values = jnp.concatenate(columns, axis=1)
            high = values.astype(jnp.bfloat16)
            rest = values - high.astype(jnp.float32)
            middle = rest.astype(jnp.bfloat16)
            low = (rest - middle.astype(jnp.float32)).astype(jnp.bfloat16)
            pieces = jnp.concatenate([high, middle, low], axis=0)
            for block in range(count):
                base = block * rows
                hit = lax.broadcasted_iota(jnp.int32, (rows, LANES), 0) + base == local_rows[table : table + 1]
                onehot = jnp.where(hit, jnp.float32(1), jnp.float32(0)).astype(jnp.bfloat16)
                onehot = jnp.concatenate([onehot] * 3, axis=1)
                row_grads = jnp.dot(onehot, pieces, preferred_element_type=jnp.float32)
                squares = jnp.sum(row_grads * row_grads, axis=1, keepdims=True)
                for start in range(0, rows, LANES):
                    place = pl.ds(base + start, LANES)
                    square = turn(squares[start : start + LANES], diagonal)
                    accum = accums_ref[table : table + 1, place] + square * (1.0 / width)
                    new_accums_ref[table : table + 1, place] = accum
                    scale = turn(learning_rate / (jnp.sqrt(accum) + epsilon), diagonal)
                    step = row_grads[start : start + LANES] * scale
                    done_ref[table, place, :] = tables_ref[table, place, :] - step
                place = pl.ds(base, rows)
                copies.append(
                    pltpu.make_async_copy(
                        done_ref.at[table, place],
                        new_tables_hbm.at[table, place],
                        sems.at[table * count + block],
                    )
                )
                copies[-1].start()
        for copy in copies:
            copy.wait()

    return call(
        body,
        "apply_update",
        [f32(*tables.shape), f32(*accums.shape)],
        [IN_VMEM] * 4,
        [IN_HBM, IN_VMEM],
        [pltpu.VMEM(tables.shape, jnp.float32), pltpu.SemaphoreType.DMA((2 * count,))],
    )(kept, swapped, tables, accums)


def local(lookup_grads, slot_index, unique_rows, tables, accums):
    n_group = lax.axis_size("group")
    n_local = lax.axis_size("local")

    def send(value, step):
        return lax.ppermute(value, AXES, ring_pairs(n_group, n_local, step))

    far0, far1, grads, codes = first_sums(slot_index, lookup_grads, [(0, 2), (1, 2)])
    far0 = send(far0, 1)
    far1 = send(far1, -1)
    back0, next1 = slot_sums(codes, grads, [(0, 3), (1, 1)])
    next1 = send(next1, 1)
    back0 = send(back0, -1)
    next0, back1 = slot_sums(codes, grads, [(0, 1), (1, 3)])
    next0 = send(next0 + far0, 1)
    back1 = send(back1 + far1, -1)
    own0, own1 = slot_sums(codes, grads, [(0, 0), (1, 0)])

    spread = finish_first_ring(unique_rows, own0, back0, next0, own1, next1, back1)
    spread = lax.all_to_all(
        spread,
        AXES,
        split_axis=0,
        concat_axis=0,
        axis_index_groups=second_groups(n_group, n_local),
        tiled=True,
    )
    kept, given = finish_second_ring(spread)

    swapped = lax.ppermute(given, "group", [(i, i ^ 1) for i in range(n_group)])
    new_tables, new_accums = apply_update(kept, swapped, tables, accums)
    return (new_tables, new_accums)


def solution(mesh):
    return jax.shard_map(
        local,
        mesh=mesh,
        in_specs=(
            P(("group", "local"), None),
            P(None, ("group", "local")),
            P(None, ("group", "local")),
            P(None, ("group", "local"), None),
            P(None, ("group", "local")),
        ),
        out_specs=(P(None, ("group", "local"), None), P(None, ("group", "local"))),
        check_vma=False,
    )
```

```python
import jax
import jax.numpy as jnp
from jax import lax
from jax.experimental import pallas as pl
from jax.experimental.pallas import tpu as pltpu
from jax.sharding import PartitionSpec as P

learning_rate = 0.1
epsilon = 1e-08

AXES = ("group", "local")
SIDE = 4
CORES = 2
LANES = 128
VMEM_BYTES = 16 << 20
FIRST_BLOCKS = (1024, 3072, 4096)
BLOCK = 1024
IN_VMEM = pl.BlockSpec(memory_space=pltpu.VMEM)
IN_HBM = pl.BlockSpec(memory_space=pltpu.HBM)


def ring_pairs(n_group, n_local, step):
    pairs = []
    for group in range(n_group):
        for place in range(n_local):
            z, x = divmod(place, SIDE)
            if group % CORES == 0:
                x = (x + step) % SIDE
            else:
                z = (z + step) % SIDE
            pairs.append((group * n_local + place, group * n_local + z * SIDE + x))
    return pairs


def position():
    group = lax.axis_index("group")
    place = lax.axis_index("local")
    z, x = lax.shift_right_logical(place, 2), place & (SIDE - 1)
    even = group & (CORES - 1) == 0
    return group, jnp.where(even, x, z), jnp.where(even, z, x), even


def second_groups(n_group, n_local):
    groups = []
    for core in range(CORES):
        for first in range(SIDE):
            members = []
            for chip in range(n_group // CORES):
                for second in range(SIDE):
                    z, x = (second, first) if core == 0 else (first, second)
                    members.append((chip * CORES + core) * n_local + z * SIDE + x)
            groups.append(members)
    return groups


def call(body, name, out_shape, in_specs, out_specs=None, scratch=(), cost=None):
    return pl.pallas_call(
        body,
        out_shape=out_shape,
        in_specs=in_specs,
        out_specs=[IN_VMEM] * len(out_shape) if out_specs is None else out_specs,
        scratch_shapes=scratch,
        compiler_params=pltpu.CompilerParams(vmem_limit_bytes=VMEM_BYTES),
        cost_estimate=cost,
        name=name,
    )


def f32(*shape):
    return jax.ShapeDtypeStruct(shape, jnp.float32)


def kernel_cost(rows, count, width):
    return pl.CostEstimate(
        flops=4 * rows * count * width // 10, bytes_accessed=count * width // 5, transcendentals=0
    )


def add_block(codes, grads, targets, start, out_refs):
    rows = out_refs[0].shape[0]
    for (table, offset), out_ref in zip(targets, out_refs):
        target = lax.broadcasted_iota(jnp.int32, (rows, grads.shape[0]), 0) + offset * rows
        hit = target == codes[table : table + 1]
        onehot = jnp.where(hit, jnp.float32(1), jnp.float32(0)).astype(jnp.bfloat16)
        piece = jnp.dot(onehot, grads, preferred_element_type=jnp.float32)
        if start == 0:
            out_ref[...] = piece
        else:
            out_ref[...] += piece


def first_sums(slot_index, lookup_grads, targets):
    count, width = lookup_grads.shape
    rows = SIDE * LANES
    blocks = len(FIRST_BLOCKS)
    pieces = [pl.ds(sum(FIRST_BLOCKS[:i]), FIRST_BLOCKS[i]) for i in range(blocks)]

    def body(index_hbm, grads_hbm, *refs):
        out_refs = refs[: len(targets)]
        grads_ref, codes_ref, index_ref, sems = refs[len(targets) :]
        index_copy = pltpu.make_async_copy(index_hbm, index_ref, sems.at[blocks])
        index_copy.start()
        copies = []
        for i, piece in enumerate(pieces):
            copies.append(
                pltpu.make_async_copy(grads_hbm.at[piece], grads_ref.at[piece], sems.at[i])
            )
        for copy in copies:
            copy.start()
        _, own_first, _, even = position()
        index_copy.wait()
        index = index_ref[...]
        first = lax.shift_right_logical(index, jnp.where(even, 7, 9)) & (SIDE - 1)
        second = lax.shift_right_logical(index, jnp.where(even, 9, 7)) & (SIDE - 1)
        first = (first - own_first) & (SIDE - 1)
        codes_ref[...] = first * rows + second * LANES + (index & (LANES - 1))
        for i, piece in enumerate(pieces):
            copies[i].wait()
            add_block(codes_ref[:, piece], grads_ref[piece, :], targets, i, out_refs)

    return call(
        body,
        "first_sums",
        [
            *[f32(rows, width) for _ in targets],
            jax.ShapeDtypeStruct(lookup_grads.shape, lookup_grads.dtype),
            jax.ShapeDtypeStruct(slot_index.shape, jnp.int32),
        ],
        [IN_HBM, IN_HBM],
        scratch=[
            pltpu.VMEM(slot_index.shape, jnp.int32),
            pltpu.SemaphoreType.DMA((blocks + 1,)),
        ],
        cost=kernel_cost(rows, count, width),
    )(
        pltpu.with_memory_space_constraint(slot_index, pltpu.HBM),
        pltpu.with_memory_space_constraint(lookup_grads, pltpu.HBM),
    )


def slot_sums(codes, lookup_grads, targets):
    count, width = lookup_grads.shape
    rows = SIDE * LANES
    block = BLOCK

    def body(codes_ref, grads_ref, *out_refs):
        for start in range(0, count, block):
            piece = pl.ds(start, block)
            add_block(codes_ref[:, piece], grads_ref[piece, :], targets, start, out_refs)

    return call(
        body,
        "slot_sums",
        [f32(rows, width) for _ in targets],
        [IN_VMEM] * 2,
        cost=kernel_cost(rows, count, width),
    )(codes, lookup_grads)


def finish_first_ring(unique_rows, own0, back0, next0, own1, next1, back1):
    rows, width = own0.shape
    chips = SIDE
    block = rows // SIDE // chips
    tiles = 2 * width // LANES

    def body(unique_ref, o0, b0, n0, o1, n1, b1, spread):
        own_second = position()[2]
        numbers = unique_ref[...].astype(jnp.float32) + 1.0
        numbers = jnp.concatenate([numbers, jnp.zeros((6, LANES), jnp.float32)], axis=0)
        for second in range(SIDE):
            mine = jnp.where(own_second == second, numbers, 0.0)
            for chip in range(chips):
                member = chip * SIDE + second
                piece = pl.ds((second * chips + chip) * block, block)
                for table, refs in enumerate([(o0, b0, n0), (o1, n1, b1)]):
                    total = refs[0][piece, :] + refs[1][piece, :] + refs[2][piece, :]
                    for tile in range(tiles // 2):
                        spot = pl.ds((table * (tiles // 2) + tile) * block, block)
                        spread[member, spot, :] = total[:, tile * LANES : (tile + 1) * LANES]
                spread[member, pl.ds(tiles * block, 8), :] = mine

    return call(
        body,
        "finish_first_ring",
        [f32(SIDE * chips, tiles * block + 8, LANES)],
        [IN_VMEM] * 7,
    )(unique_rows, own0, back0, next0, own1, next1, back1)[0]


def finish_second_ring(spread):
    members, rows, lanes = spread.shape
    chips = members // SIDE
    half = LANES // 8
    tiles = (rows - 8) // (CORES * half)

    def body(spread_ref, kept, given):
        even = position()[3]

        def total(chip, piece):
            pieces = [spread_ref[chip * SIDE + second, piece, :] for second in range(SIDE)]
            return (pieces[0] + pieces[1]) + (pieces[2] + pieces[3])

        for chip in range(chips):
            for tile in range(tiles):
                low = total(chip, pl.ds(tile * CORES * half, half))
                high = total(chip, pl.ds(tile * CORES * half + half, half))
                spot = pl.ds(tile * half, half)
                kept[chip, spot, :] = jnp.where(even, low, high)
                given[chip, spot, :] = jnp.where(even, high, low)
            numbers = total(chip, pl.ds(rows - 8, 8))
            kept[chip, pl.ds(tiles * half, 8), :] = numbers
            given[chip, pl.ds(tiles * half, 8), :] = numbers

    return call(
        body, "finish_second_ring", [f32(chips, tiles * half + 8, lanes)] * 2, [IN_VMEM]
    )(spread)


def eye():
    shape = (LANES, LANES)
    return lax.broadcasted_iota(jnp.int32, shape, 0) == lax.broadcasted_iota(jnp.int32, shape, 1)


def turn(vector, diagonal):
    axis = 1 if vector.shape[0] == 1 else 0
    square = jnp.where(diagonal, jnp.broadcast_to(vector, (LANES, LANES)), 0.0)
    return jnp.sum(square, axis=axis, keepdims=True)


def apply_update(kept, swapped, tables, accums):
    rows_dev, width = tables.shape[1:]
    rows = 256
    count = rows_dev // rows

    chips, slots = kept.shape[:2]
    bucket = LANES // (CORES * chips)
    slots -= 8
    tiles = width // LANES

    def body(kept_ref, swapped_ref, tables_ref, accums_ref, *refs):
        new_tables_hbm, new_accums_ref, done_ref, sems = refs
        diagonal = eye()
        copies = []
        sources = [(ref, chip) for ref in (kept_ref, swapped_ref) for chip in range(chips)]
        group = position()[0]
        lane = lax.broadcasted_iota(jnp.int32, (8, LANES), 1) // bucket
        local_rows = jnp.zeros((8, LANES), jnp.int32)
        for spot, (ref, chip) in enumerate(sources):
            listed = ref[chip, pl.ds(slots, 8), :].astype(jnp.int32)
            listed = pltpu.roll(listed, ((spot - group) * bucket) & (LANES - 1), 1)
            local_rows = jnp.where(lane == spot, listed, local_rows)
        local_rows = jnp.where(local_rows == 0, -1, (local_rows - 1) & (rows_dev - 1))
        for table in range(2):
            columns = []
            for tile in range(table * tiles, (table + 1) * tiles):
                spot = pl.ds(tile * bucket, bucket)
                columns.append(jnp.concatenate([ref[chip, spot, :] for ref, chip in sources]))
            values = jnp.concatenate(columns, axis=1)
            high = values.astype(jnp.bfloat16)
            rest = values - high.astype(jnp.float32)
            middle = rest.astype(jnp.bfloat16)
            low = (rest - middle.astype(jnp.float32)).astype(jnp.bfloat16)
            pieces = jnp.concatenate([high, middle, low], axis=0)
            for block in range(count):
                base = block * rows
                hit = lax.broadcasted_iota(jnp.int32, (rows, LANES), 0) + base == local_rows[table : table + 1]
                onehot = jnp.where(hit, jnp.float32(1), jnp.float32(0)).astype(jnp.bfloat16)
                onehot = jnp.concatenate([onehot] * 3, axis=1)
                row_grads = jnp.dot(onehot, pieces, preferred_element_type=jnp.float32)
                squares = jnp.sum(row_grads * row_grads, axis=1, keepdims=True)
                for start in range(0, rows, LANES):
                    place = pl.ds(base + start, LANES)
                    square = turn(squares[start : start + LANES], diagonal)
                    accum = accums_ref[table : table + 1, place] + square * (1.0 / width)
                    new_accums_ref[table : table + 1, place] = accum
                    scale = turn(learning_rate / (jnp.sqrt(accum) + epsilon), diagonal)
                    step = row_grads[start : start + LANES] * scale
                    done_ref[table, place, :] = tables_ref[table, place, :] - step
                place = pl.ds(base, rows)
                copies.append(
                    pltpu.make_async_copy(
                        done_ref.at[table, place],
                        new_tables_hbm.at[table, place],
                        sems.at[table * count + block],
                    )
                )
                copies[-1].start()
        for copy in copies:
            copy.wait()

    return call(
        body,
        "apply_update",
        [f32(*tables.shape), f32(*accums.shape)],
        [IN_VMEM] * 4,
        [IN_HBM, IN_VMEM],
        [pltpu.VMEM(tables.shape, jnp.float32), pltpu.SemaphoreType.DMA((2 * count,))],
    )(kept, swapped, tables, accums)


def local(lookup_grads, slot_index, unique_rows, tables, accums):
    n_group = lax.axis_size("group")
    n_local = lax.axis_size("local")

    def send(value, step):
        return lax.ppermute(value, AXES, ring_pairs(n_group, n_local, step))

    far0, far1, grads, codes = first_sums(slot_index, lookup_grads, [(0, 2), (1, 2)])
    far0 = send(far0, 1)
    far1 = send(far1, -1)
    back0, next1 = slot_sums(codes, grads, [(0, 3), (1, 1)])
    next1 = send(next1, 1)
    back0 = send(back0, -1)
    next0, back1 = slot_sums(codes, grads, [(0, 1), (1, 3)])
    next0 = send(next0 + far0, 1)
    back1 = send(back1 + far1, -1)
    own0, own1 = slot_sums(codes, grads, [(0, 0), (1, 0)])

    spread = finish_first_ring(unique_rows, own0, back0, next0, own1, next1, back1)
    spread = lax.all_to_all(
        spread,
        AXES,
        split_axis=0,
        concat_axis=0,
        axis_index_groups=second_groups(n_group, n_local),
        tiled=True,
    )
    kept, given = finish_second_ring(spread)

    swapped = lax.ppermute(given, "group", [(i, i ^ 1) for i in range(n_group)])
    new_tables, new_accums = apply_update(kept, swapped, tables, accums)
    return (new_tables, new_accums)


def solution(mesh):
    return jax.shard_map(
        local,
        mesh=mesh,
        in_specs=(
            P(("group", "local"), None),
            P(None, ("group", "local")),
            P(None, ("group", "local")),
            P(None, ("group", "local"), None),
            P(None, ("group", "local")),
        ),
        out_specs=(P(None, ("group", "local"), None), P(None, ("group", "local"))),
        check_vma=False,
    )
```

```python
import jax
import jax.numpy as jnp
from jax import lax
from jax.experimental import pallas as pl
from jax.experimental.pallas import tpu as pltpu
from jax.sharding import PartitionSpec as P

learning_rate = 0.1
epsilon = 1e-08

AXES = ("group", "local")
SIDE = 4
CORES = 2
LANES = 128
VMEM_BYTES = 16 << 20
FIRST_BLOCKS = (1024, 3072, 4096)
BLOCK = 1024
IN_VMEM = pl.BlockSpec(memory_space=pltpu.VMEM)
IN_HBM = pl.BlockSpec(memory_space=pltpu.HBM)


def ring_pairs(n_group, n_local, ring, step):
    pairs = []
    for group in range(n_group):
        for place in range(n_local):
            z, x = divmod(place, SIDE)
            if (group + ring) % CORES == 0:
                x = (x + step) % SIDE
            else:
                z = (z + step) % SIDE
            pairs.append((group * n_local + place, group * n_local + z * SIDE + x))
    return pairs


def position():
    group = lax.axis_index("group")
    place = lax.axis_index("local")
    z, x = lax.shift_right_logical(place, 2), place & (SIDE - 1)
    even = group & (CORES - 1) == 0
    return group, jnp.where(even, x, z), jnp.where(even, z, x), even


def call(body, name, out_shape, in_specs, out_specs=None, scratch=(), cost=None):
    return pl.pallas_call(
        body,
        out_shape=out_shape,
        in_specs=in_specs,
        out_specs=[IN_VMEM] * len(out_shape) if out_specs is None else out_specs,
        scratch_shapes=scratch,
        compiler_params=pltpu.CompilerParams(vmem_limit_bytes=VMEM_BYTES),
        cost_estimate=cost,
        name=name,
    )


def f32(*shape):
    return jax.ShapeDtypeStruct(shape, jnp.float32)


def kernel_cost(rows, count, width):
    return pl.CostEstimate(
        flops=4 * rows * count * width // 10, bytes_accessed=count * width // 5, transcendentals=0
    )


def add_block(codes, grads, targets, start, out_refs):
    rows = out_refs[0].shape[0]
    for (table, offset), out_ref in zip(targets, out_refs):
        target = lax.broadcasted_iota(jnp.int32, (rows, grads.shape[0]), 0) + offset * rows
        hit = target == codes[table : table + 1]
        onehot = jnp.where(hit, jnp.float32(1), jnp.float32(0)).astype(jnp.bfloat16)
        piece = jnp.dot(onehot, grads, preferred_element_type=jnp.float32)
        if start == 0:
            out_ref[...] = piece
        else:
            out_ref[...] += piece


def first_sums(slot_index, lookup_grads, targets):
    count, width = lookup_grads.shape
    rows = SIDE * LANES
    blocks = len(FIRST_BLOCKS)
    pieces = [pl.ds(sum(FIRST_BLOCKS[:i]), FIRST_BLOCKS[i]) for i in range(blocks)]

    def body(index_hbm, grads_hbm, *refs):
        out_refs = refs[: len(targets)]
        grads_ref, codes_ref, index_ref, sems = refs[len(targets) :]
        index_copy = pltpu.make_async_copy(index_hbm, index_ref, sems.at[blocks])
        index_copy.start()
        copies = []
        for i, piece in enumerate(pieces):
            copies.append(
                pltpu.make_async_copy(grads_hbm.at[piece], grads_ref.at[piece], sems.at[i])
            )
        for copy in copies:
            copy.start()
        _, own_first, own_second, even = position()
        index_copy.wait()
        index = index_ref[...]
        first = lax.shift_right_logical(index, jnp.where(even, 7, 9)) & (SIDE - 1)
        second = lax.shift_right_logical(index, jnp.where(even, 9, 7)) & (SIDE - 1)
        first = (first - own_first) & (SIDE - 1)
        second = (second - own_second) & (SIDE - 1)
        codes_ref[...] = first * rows + second * LANES + (index & (LANES - 1))
        for i, piece in enumerate(pieces):
            copies[i].wait()
            add_block(codes_ref[:, piece], grads_ref[piece, :], targets, i, out_refs)

    return call(
        body,
        "first_sums",
        [
            *[f32(rows, width) for _ in targets],
            jax.ShapeDtypeStruct(lookup_grads.shape, lookup_grads.dtype),
            jax.ShapeDtypeStruct(slot_index.shape, jnp.int32),
        ],
        [IN_HBM, IN_HBM],
        scratch=[
            pltpu.VMEM(slot_index.shape, jnp.int32),
            pltpu.SemaphoreType.DMA((blocks + 1,)),
        ],
        cost=kernel_cost(rows, count, width),
    )(
        pltpu.with_memory_space_constraint(slot_index, pltpu.HBM),
        pltpu.with_memory_space_constraint(lookup_grads, pltpu.HBM),
    )


def slot_sums(codes, lookup_grads, targets, after):
    count, width = lookup_grads.shape
    rows = SIDE * LANES
    block = BLOCK

    def body(codes_ref, grads_ref, after_ref, *out_refs):
        for start in range(0, count, block):
            piece = pl.ds(start, block)
            add_block(codes_ref[:, piece], grads_ref[piece, :], targets, start, out_refs)

    return call(
        body,
        "slot_sums",
        [f32(rows, width) for _ in targets],
        [IN_VMEM] * 3,
        cost=kernel_cost(rows, count, width),
    )(codes, lookup_grads, after)


def finish_first_ring(token, own0, back0, next0, own1, next1, back1):
    rows, width = own0.shape
    slots = rows // SIDE

    def body(token_ref, o0, b0, n0, o1, n1, b1, *out_refs):
        for offset in range(SIDE):
            piece = pl.ds(offset * slots, slots)
            for table, refs in enumerate([(o0, b0, n0), (o1, n1, b1)]):
                total = refs[0][piece, :] + refs[1][piece, :] + refs[2][piece, :]
                out_refs[offset][pl.ds(table * slots, slots), :] = total

    return call(body, "finish_first_ring", [f32(2 * slots, width)] * SIDE, [IN_VMEM] * 7)(
        token, own0, back0, next0, own1, next1, back1
    )


def finish_second_ring(unique_rows, pieces):
    rows, width = pieces[0].shape
    slots = rows // 2
    chips = SIDE
    bucket = slots // (CORES * chips)
    height = 2 * bucket + 8

    def body(unique_ref, p0, p1, p2, p3, kept, given):
        group = position()[0]
        core = group & (CORES - 1)
        numbers = unique_ref[...].astype(jnp.float32) + 1.0
        for offset in range(chips):
            chip = (lax.shift_right_logical(group, 1) + offset) & (chips - 1)
            for out_ref, owner in [(kept, core), (given, 1 - core)]:
                for table in range(2):
                    start = table * slots + (chip * CORES + owner) * bucket
                    piece = pl.ds(pl.multiple_of(start, bucket), bucket)
                    total = (p0[piece, :] + p1[piece, :]) + (p2[piece, :] + p3[piece, :])
                    out_ref[offset, pl.ds(table * bucket, bucket), :] = total
                out_ref[offset, pl.ds(2 * bucket, 8), :] = jnp.zeros((8, width), jnp.float32)
                out_ref[offset, pl.ds(2 * bucket, 2), pl.ds(0, LANES)] = numbers

    return call(
        body, "finish_second_ring", [f32(chips, height, width)] * 2, [IN_VMEM] * (1 + SIDE)
    )(unique_rows, *pieces)


def eye():
    shape = (LANES, LANES)
    return lax.broadcasted_iota(jnp.int32, shape, 0) == lax.broadcasted_iota(jnp.int32, shape, 1)


def turn(vector, diagonal):
    axis = 1 if vector.shape[0] == 1 else 0
    square = jnp.where(diagonal, jnp.broadcast_to(vector, (LANES, LANES)), 0.0)
    return jnp.sum(square, axis=axis, keepdims=True)


def apply_update(arrived, tables, accums):
    rows_dev, width = tables.shape[1:]
    rows = 256
    count = rows_dev // rows
    height = arrived[0].shape[0] // CORES
    bucket = (height - 8) // 2

    def body(*refs):
        arrived_refs = refs[:SIDE]
        tables_ref, accums_ref, new_tables_hbm, new_accums_ref, done_ref, sems = refs[SIDE:]
        diagonal = eye()
        copies = []
        sources = [(ref, core * height) for ref in arrived_refs for core in range(CORES)]
        group = position()[0]
        lane = lax.broadcasted_iota(jnp.int32, (8, LANES), 1) // bucket
        local_rows = jnp.zeros((8, LANES), jnp.int32)
        for spot, (ref, first) in enumerate(sources):
            listed = ref[pl.ds(first + 2 * bucket, 8), pl.ds(0, LANES)].astype(jnp.int32)
            listed = pltpu.roll(listed, ((spot - group) * bucket) & (LANES - 1), 1)
            local_rows = jnp.where(lane == spot, listed, local_rows)
        local_rows = jnp.where(local_rows == 0, -1, (local_rows - 1) & (rows_dev - 1))
        for table in range(2):
            values = jnp.concatenate(
                [ref[pl.ds(first + table * bucket, bucket), :] for ref, first in sources]
            )
            high = values.astype(jnp.bfloat16)
            rest = values - high.astype(jnp.float32)
            middle = rest.astype(jnp.bfloat16)
            low = (rest - middle.astype(jnp.float32)).astype(jnp.bfloat16)
            pieces = jnp.concatenate([high, middle, low], axis=0)
            for block in range(count):
                base = block * rows
                hit = lax.broadcasted_iota(jnp.int32, (rows, LANES), 0) + base == local_rows[table : table + 1]
                onehot = jnp.where(hit, jnp.float32(1), jnp.float32(0)).astype(jnp.bfloat16)
                onehot = jnp.concatenate([onehot] * 3, axis=1)
                row_grads = jnp.dot(onehot, pieces, preferred_element_type=jnp.float32)
                squares = jnp.sum(row_grads * row_grads, axis=1, keepdims=True)
                for start in range(0, rows, LANES):
                    place = pl.ds(base + start, LANES)
                    square = turn(squares[start : start + LANES], diagonal)
                    accum = accums_ref[table : table + 1, place] + square * (1.0 / width)
                    new_accums_ref[table : table + 1, place] = accum
                    scale = turn(learning_rate / (jnp.sqrt(accum) + epsilon), diagonal)
                    step = row_grads[start : start + LANES] * scale
                    done_ref[table, place, :] = tables_ref[table, place, :] - step
                place = pl.ds(base, rows)
                copies.append(
                    pltpu.make_async_copy(
                        done_ref.at[table, place],
                        new_tables_hbm.at[table, place],
                        sems.at[table * count + block],
                    )
                )
                copies[-1].start()
        for copy in copies:
            copy.wait()

    return call(
        body,
        "apply_update",
        [f32(*tables.shape), f32(*accums.shape)],
        [IN_VMEM] * (SIDE + 2),
        [IN_HBM, IN_VMEM],
        [pltpu.VMEM(tables.shape, jnp.float32), pltpu.SemaphoreType.DMA((2 * count,))],
    )(*arrived, tables, accums)


def local(lookup_grads, slot_index, unique_rows, tables, accums):
    n_group = lax.axis_size("group")
    n_local = lax.axis_size("local")

    def send(value, step, ring=0):
        return lax.ppermute(value, AXES, ring_pairs(n_group, n_local, ring, step))

    def send_along(value, step):
        return lax.ppermute(
            value, "group", [(i, (i + CORES * step) % n_group) for i in range(n_group)]
        )

    far0, far1, grads, codes = first_sums(slot_index, lookup_grads, [(0, 2), (1, 2)])
    back0, next1 = slot_sums(codes, grads, [(0, 3), (1, 1)], far0)
    next0, back1 = slot_sums(codes, grads, [(0, 1), (1, 3)], next1)
    own0, own1 = slot_sums(codes, grads, [(0, 0), (1, 0)], back1)
    far0 = send(far0, 1)
    far1 = send(far1, -1)
    next1 = send(next1, 1)
    back0 = send(back0, -1)
    next0 = send(next0 + far0, 1)
    back1 = send(back1 + far1, -1)

    token = lax.ppermute(
        sum(value[:8, :LANES] for value in (next0, back0, next1, back1, own0)),
        "group",
        [(i, i ^ 1) for i in range(n_group)],
    )

    pieces = finish_first_ring(token, own0, back0, next0, own1, next1, back1)
    pieces = [pieces[0]] + [send(pieces[step], step, ring=1) for step in range(1, SIDE)]
    kept, given = finish_second_ring(unique_rows, pieces)

    swapped = lax.ppermute(given, "group", [(i, i ^ 1) for i in range(n_group)])
    arrived = [jnp.concatenate([kept[step], swapped[step]]) for step in range(SIDE)]
    arrived = [arrived[0]] + [send_along(arrived[step], step) for step in range(1, SIDE)]
    new_tables, new_accums = apply_update(arrived, tables, accums)
    return (new_tables, new_accums)


def solution(mesh):
    return jax.shard_map(
        local,
        mesh=mesh,
        in_specs=(
            P(("group", "local"), None),
            P(None, ("group", "local")),
            P(None, ("group", "local")),
            P(None, ("group", "local"), None),
            P(None, ("group", "local")),
        ),
        out_specs=(P(None, ("group", "local"), None), P(None, ("group", "local"))),
        check_vma=False,
    )
```

```python
import jax
import jax.numpy as jnp
from jax import lax
from jax.experimental import pallas as pl
from jax.experimental.pallas import tpu as pltpu
from jax.sharding import PartitionSpec as P

learning_rate = 0.1
epsilon = 1e-08

AXES = ("group", "local")
SIDE = 4
CORES = 2
LANES = 128
VMEM_BYTES = 16 << 20
FIRST_BLOCKS = (1024, 3072, 4096)
BLOCK = 1024
IN_VMEM = pl.BlockSpec(memory_space=pltpu.VMEM)
IN_HBM = pl.BlockSpec(memory_space=pltpu.HBM)


def ring_pairs(n_group, n_local, ring, step):
    pairs = []
    for group in range(n_group):
        for place in range(n_local):
            z, x = divmod(place, SIDE)
            if (group + ring) % CORES == 0:
                x = (x + step) % SIDE
            else:
                z = (z + step) % SIDE
            pairs.append((group * n_local + place, group * n_local + z * SIDE + x))
    return pairs


def position():
    group = lax.axis_index("group")
    place = lax.axis_index("local")
    z, x = lax.shift_right_logical(place, 2), place & (SIDE - 1)
    even = group & (CORES - 1) == 0
    return group, jnp.where(even, x, z), jnp.where(even, z, x), even


def call(body, name, out_shape, in_specs, out_specs=None, scratch=(), cost=None):
    return pl.pallas_call(
        body,
        out_shape=out_shape,
        in_specs=in_specs,
        out_specs=[IN_VMEM] * len(out_shape) if out_specs is None else out_specs,
        scratch_shapes=scratch,
        compiler_params=pltpu.CompilerParams(vmem_limit_bytes=VMEM_BYTES),
        cost_estimate=cost,
        name=name,
    )


def f32(*shape):
    return jax.ShapeDtypeStruct(shape, jnp.float32)


def kernel_cost(rows, count, width):
    return pl.CostEstimate(
        flops=4 * rows * count * width // 10, bytes_accessed=count * width // 5, transcendentals=0
    )


def add_block(codes, grads, targets, start, out_refs):
    rows = out_refs[0].shape[0]
    for (table, offset), out_ref in zip(targets, out_refs):
        target = lax.broadcasted_iota(jnp.int32, (rows, grads.shape[0]), 0) + offset * rows
        hit = target == codes[table : table + 1]
        onehot = jnp.where(hit, jnp.float32(1), jnp.float32(0)).astype(jnp.bfloat16)
        piece = jnp.dot(onehot, grads, preferred_element_type=jnp.float32)
        if start == 0:
            out_ref[...] = piece
        else:
            out_ref[...] += piece


def first_sums(slot_index, lookup_grads, targets):
    count, width = lookup_grads.shape
    rows = SIDE * LANES
    blocks = len(FIRST_BLOCKS)
    pieces = [pl.ds(sum(FIRST_BLOCKS[:i]), FIRST_BLOCKS[i]) for i in range(blocks)]

    def body(index_hbm, grads_hbm, *refs):
        out_refs = refs[: len(targets)]
        grads_ref, codes_ref, index_ref, sems = refs[len(targets) :]
        index_copy = pltpu.make_async_copy(index_hbm, index_ref, sems.at[blocks])
        index_copy.start()
        copies = []
        for i, piece in enumerate(pieces):
            copies.append(
                pltpu.make_async_copy(grads_hbm.at[piece], grads_ref.at[piece], sems.at[i])
            )
        for copy in copies:
            copy.start()
        _, own_first, own_second, even = position()
        index_copy.wait()
        index = index_ref[...]
        first = lax.shift_right_logical(index, jnp.where(even, 7, 9)) & (SIDE - 1)
        second = lax.shift_right_logical(index, jnp.where(even, 9, 7)) & (SIDE - 1)
        first = (first - own_first) & (SIDE - 1)
        second = (second - own_second) & (SIDE - 1)
        codes_ref[...] = first * rows + second * LANES + (index & (LANES - 1))
        for i, piece in enumerate(pieces):
            copies[i].wait()
            add_block(codes_ref[:, piece], grads_ref[piece, :], targets, i, out_refs)

    return call(
        body,
        "first_sums",
        [
            *[f32(rows, width) for _ in targets],
            jax.ShapeDtypeStruct(lookup_grads.shape, lookup_grads.dtype),
            jax.ShapeDtypeStruct(slot_index.shape, jnp.int32),
        ],
        [IN_HBM, IN_HBM],
        scratch=[
            pltpu.VMEM(slot_index.shape, jnp.int32),
            pltpu.SemaphoreType.DMA((blocks + 1,)),
        ],
        cost=kernel_cost(rows, count, width),
    )(
        pltpu.with_memory_space_constraint(slot_index, pltpu.HBM),
        pltpu.with_memory_space_constraint(lookup_grads, pltpu.HBM),
    )


def slot_sums(codes, lookup_grads, targets, after):
    count, width = lookup_grads.shape
    rows = SIDE * LANES
    block = BLOCK

    def body(codes_ref, grads_ref, after_ref, *out_refs):
        for start in range(0, count, block):
            piece = pl.ds(start, block)
            add_block(codes_ref[:, piece], grads_ref[piece, :], targets, start, out_refs)

    return call(
        body,
        "slot_sums",
        [f32(rows, width) for _ in targets],
        [IN_VMEM] * 3,
        cost=kernel_cost(rows, count, width),
    )(codes, lookup_grads, after)


def finish_first_ring(token, own0, back0, next0, own1, next1, back1):
    rows, width = own0.shape
    slots = rows // SIDE

    def body(token_ref, o0, b0, n0, o1, n1, b1, *out_refs):
        for offset in range(SIDE):
            piece = pl.ds(offset * slots, slots)
            for table, refs in enumerate([(o0, b0, n0), (o1, n1, b1)]):
                total = refs[0][piece, :] + refs[1][piece, :] + refs[2][piece, :]
                out_refs[offset][pl.ds(table * slots, slots), :] = total

    return call(body, "finish_first_ring", [f32(2 * slots, width)] * SIDE, [IN_VMEM] * 7)(
        token, own0, back0, next0, own1, next1, back1
    )


def finish_second_ring(unique_rows, pieces):
    rows, width = pieces[0].shape
    slots = rows // 2
    chips = SIDE
    bucket = slots // (CORES * chips)
    height = 2 * bucket + 8

    def body(unique_ref, p0, p1, p2, p3, kept, given):
        group = position()[0]
        core = group & (CORES - 1)
        numbers = unique_ref[...].astype(jnp.float32) + 1.0
        for offset in range(chips):
            chip = (lax.shift_right_logical(group, 1) + offset) & (chips - 1)
            for out_ref, owner in [(kept, core), (given, 1 - core)]:
                for table in range(2):
                    start = table * slots + (chip * CORES + owner) * bucket
                    piece = pl.ds(pl.multiple_of(start, bucket), bucket)
                    total = (p0[piece, :] + p1[piece, :]) + (p2[piece, :] + p3[piece, :])
                    out_ref[offset, pl.ds(table * bucket, bucket), :] = total
                out_ref[offset, pl.ds(2 * bucket, 8), :] = jnp.zeros((8, width), jnp.float32)
                out_ref[offset, pl.ds(2 * bucket, 2), pl.ds(0, LANES)] = numbers

    return call(
        body, "finish_second_ring", [f32(chips, height, width)] * 2, [IN_VMEM] * (1 + SIDE)
    )(unique_rows, *pieces)


def eye():
    shape = (LANES, LANES)
    return lax.broadcasted_iota(jnp.int32, shape, 0) == lax.broadcasted_iota(jnp.int32, shape, 1)


def turn(vector, diagonal):
    axis = 1 if vector.shape[0] == 1 else 0
    square = jnp.where(diagonal, jnp.broadcast_to(vector, (LANES, LANES)), 0.0)
    return jnp.sum(square, axis=axis, keepdims=True)


def apply_update(arrived, tables, accums):
    rows_dev, width = tables.shape[1:]
    rows = 256
    count = rows_dev // rows
    height = arrived[0].shape[0] // CORES
    bucket = (height - 8) // 2

    def body(*refs):
        arrived_refs = refs[:SIDE]
        tables_ref, accums_ref, new_tables_hbm, new_accums_ref, done_ref, sems = refs[SIDE:]
        diagonal = eye()
        copies = []
        sources = [(ref, core * height) for ref in arrived_refs for core in range(CORES)]
        group = position()[0]
        lane = lax.broadcasted_iota(jnp.int32, (8, LANES), 1) // bucket
        local_rows = jnp.zeros((8, LANES), jnp.int32)
        for spot, (ref, first) in enumerate(sources):
            listed = ref[pl.ds(first + 2 * bucket, 8), pl.ds(0, LANES)].astype(jnp.int32)
            listed = pltpu.roll(listed, ((spot - group) * bucket) & (LANES - 1), 1)
            local_rows = jnp.where(lane == spot, listed, local_rows)
        local_rows = jnp.where(local_rows == 0, -1, (local_rows - 1) & (rows_dev - 1))
        for table in range(2):
            values = jnp.concatenate(
                [ref[pl.ds(first + table * bucket, bucket), :] for ref, first in sources]
            )
            high = values.astype(jnp.bfloat16)
            rest = values - high.astype(jnp.float32)
            middle = rest.astype(jnp.bfloat16)
            low = (rest - middle.astype(jnp.float32)).astype(jnp.bfloat16)
            pieces = jnp.concatenate([high, middle, low], axis=0)
            for block in range(count):
                base = block * rows
                hit = lax.broadcasted_iota(jnp.int32, (rows, LANES), 0) + base == local_rows[table : table + 1]
                onehot = jnp.where(hit, jnp.float32(1), jnp.float32(0)).astype(jnp.bfloat16)
                onehot = jnp.concatenate([onehot] * 3, axis=1)
                row_grads = jnp.dot(onehot, pieces, preferred_element_type=jnp.float32)
                squares = jnp.sum(row_grads * row_grads, axis=1, keepdims=True)
                for start in range(0, rows, LANES):
                    place = pl.ds(base + start, LANES)
                    square = turn(squares[start : start + LANES], diagonal)
                    accum = accums_ref[table : table + 1, place] + square * (1.0 / width)
                    new_accums_ref[table : table + 1, place] = accum
                    scale = turn(learning_rate / (jnp.sqrt(accum) + epsilon), diagonal)
                    step = row_grads[start : start + LANES] * scale
                    done_ref[table, place, :] = tables_ref[table, place, :] - step
                place = pl.ds(base, rows)
                copies.append(
                    pltpu.make_async_copy(
                        done_ref.at[table, place],
                        new_tables_hbm.at[table, place],
                        sems.at[table * count + block],
                    )
                )
                copies[-1].start()
        for copy in copies:
            copy.wait()

    return call(
        body,
        "apply_update",
        [f32(*tables.shape), f32(*accums.shape)],
        [IN_VMEM] * (SIDE + 2),
        [IN_HBM, IN_VMEM],
        [pltpu.VMEM(tables.shape, jnp.float32), pltpu.SemaphoreType.DMA((2 * count,))],
    )(*arrived, tables, accums)


def local(lookup_grads, slot_index, unique_rows, tables, accums):
    n_group = lax.axis_size("group")
    n_local = lax.axis_size("local")

    def send(value, step, ring=0):
        return lax.ppermute(value, AXES, ring_pairs(n_group, n_local, ring, step))

    def send_along(value, step):
        return lax.ppermute(
            value, "group", [(i, (i + CORES * step) % n_group) for i in range(n_group)]
        )

    far0, far1, grads, codes = first_sums(slot_index, lookup_grads, [(0, 2), (1, 2)])
    back0, next1 = slot_sums(codes, grads, [(0, 3), (1, 1)], far0)
    next0, back1 = slot_sums(codes, grads, [(0, 1), (1, 3)], next1)
    own0, own1 = slot_sums(codes, grads, [(0, 0), (1, 0)], back1)
    far0 = send(far0, 1)
    far1 = send(far1, -1)
    next1 = send(next1, 1)
    back0 = send(back0, -1)
    next0 = send(next0 + far0, 1)
    back1 = send(back1 + far1, -1)

    token = lax.ppermute(
        sum(value[:8, :LANES] for value in (next0, back0, next1, back1, own0)),
        "group",
        [(i, i ^ 1) for i in range(n_group)],
    )

    pieces = finish_first_ring(token, own0, back0, next0, own1, next1, back1)
    pieces = [pieces[0]] + [send(pieces[step], step, ring=1) for step in (2, 1, 3)]
    kept, given = finish_second_ring(unique_rows, pieces)

    swapped = lax.ppermute(given, "group", [(i, i ^ 1) for i in range(n_group)])
    arrived = [jnp.concatenate([kept[step], swapped[step]]) for step in range(SIDE)]
    arrived = [arrived[0]] + [send_along(arrived[step], step) for step in (2, 1, 3)]
    new_tables, new_accums = apply_update(arrived, tables, accums)
    return (new_tables, new_accums)


def solution(mesh):
    return jax.shard_map(
        local,
        mesh=mesh,
        in_specs=(
            P(("group", "local"), None),
            P(None, ("group", "local")),
            P(None, ("group", "local")),
            P(None, ("group", "local"), None),
            P(None, ("group", "local")),
        ),
        out_specs=(P(None, ("group", "local"), None), P(None, ("group", "local"))),
        check_vma=False,
    )
```

```python
import jax
import jax.numpy as jnp
from jax import lax
from jax.experimental import pallas as pl
from jax.experimental.pallas import tpu as pltpu
from jax.sharding import PartitionSpec as P

learning_rate = 0.1
epsilon = 1e-08

AXES = ("group", "local")
SIDE = 4
CORES = 2
LANES = 128
VMEM_BYTES = 16 << 20
FIRST_BLOCKS = (512, 1536, 2048, 4096)
BLOCK = 1024
IN_VMEM = pl.BlockSpec(memory_space=pltpu.VMEM)
IN_HBM = pl.BlockSpec(memory_space=pltpu.HBM)


def ring_pairs(n_group, n_local, ring, step):
    pairs = []
    for group in range(n_group):
        for place in range(n_local):
            z, x = divmod(place, SIDE)
            if (group + ring) % CORES == 0:
                x = (x + step) % SIDE
            else:
                z = (z + step) % SIDE
            pairs.append((group * n_local + place, group * n_local + z * SIDE + x))
    return pairs


def position():
    group = lax.axis_index("group")
    place = lax.axis_index("local")
    z, x = lax.shift_right_logical(place, 2), place & (SIDE - 1)
    even = group & (CORES - 1) == 0
    return group, jnp.where(even, x, z), jnp.where(even, z, x), even


def call(body, name, out_shape, in_specs, out_specs=None, scratch=(), cost=None):
    return pl.pallas_call(
        body,
        out_shape=out_shape,
        in_specs=in_specs,
        out_specs=[IN_VMEM] * len(out_shape) if out_specs is None else out_specs,
        scratch_shapes=scratch,
        compiler_params=pltpu.CompilerParams(vmem_limit_bytes=VMEM_BYTES),
        cost_estimate=cost,
        name=name,
    )


def f32(*shape):
    return jax.ShapeDtypeStruct(shape, jnp.float32)


def kernel_cost(rows, count, width):
    return pl.CostEstimate(
        flops=4 * rows * count * width // 10, bytes_accessed=count * width // 5, transcendentals=0
    )


def add_block(codes, grads, targets, start, out_refs):
    rows = out_refs[0].shape[0]
    for (table, offset), out_ref in zip(targets, out_refs):
        target = lax.broadcasted_iota(jnp.int32, (rows, grads.shape[0]), 0) + offset * rows
        hit = target == codes[table : table + 1]
        onehot = jnp.where(hit, jnp.float32(1), jnp.float32(0)).astype(jnp.bfloat16)
        piece = jnp.dot(onehot, grads, preferred_element_type=jnp.float32)
        if start == 0:
            out_ref[...] = piece
        else:
            out_ref[...] += piece


def first_sums(slot_index, lookup_grads, targets):
    count, width = lookup_grads.shape
    rows = SIDE * LANES
    blocks = len(FIRST_BLOCKS)
    pieces = [pl.ds(sum(FIRST_BLOCKS[:i]), FIRST_BLOCKS[i]) for i in range(blocks)]

    def body(index_hbm, grads_hbm, *refs):
        out_refs = refs[: len(targets)]
        grads_ref, codes_ref, index_ref, sems = refs[len(targets) :]
        index_copy = pltpu.make_async_copy(index_hbm, index_ref, sems.at[blocks])
        index_copy.start()
        copies = []
        for i, piece in enumerate(pieces):
            copies.append(
                pltpu.make_async_copy(grads_hbm.at[piece], grads_ref.at[piece], sems.at[i])
            )
        for copy in copies:
            copy.start()
        _, own_first, own_second, even = position()
        index_copy.wait()
        for i, piece in enumerate(pieces):
            index = index_ref[:, piece]
            first = lax.shift_right_logical(index, jnp.where(even, 7, 9)) & (SIDE - 1)
            second = lax.shift_right_logical(index, jnp.where(even, 9, 7)) & (SIDE - 1)
            first = (first - own_first) & (SIDE - 1)
            second = (second - own_second) & (SIDE - 1)
            codes = first * rows + second * LANES + (index & (LANES - 1))
            codes_ref[:, piece] = codes
            copies[i].wait()
            add_block(codes, grads_ref[piece, :], targets, i, out_refs)

    return call(
        body,
        "first_sums",
        [
            *[f32(rows, width) for _ in targets],
            jax.ShapeDtypeStruct(lookup_grads.shape, lookup_grads.dtype),
            jax.ShapeDtypeStruct(slot_index.shape, jnp.int32),
        ],
        [IN_HBM, IN_HBM],
        scratch=[
            pltpu.VMEM(slot_index.shape, jnp.int32),
            pltpu.SemaphoreType.DMA((blocks + 1,)),
        ],
        cost=kernel_cost(rows, count, width),
    )(
        pltpu.with_memory_space_constraint(slot_index, pltpu.HBM),
        pltpu.with_memory_space_constraint(lookup_grads, pltpu.HBM),
    )


def slot_sums(codes, lookup_grads, targets, after):
    count, width = lookup_grads.shape
    rows = SIDE * LANES
    block = BLOCK

    def body(codes_ref, grads_ref, after_ref, *out_refs):
        for start in range(0, count, block):
            piece = pl.ds(start, block)
            add_block(codes_ref[:, piece], grads_ref[piece, :], targets, start, out_refs)

    return call(
        body,
        "slot_sums",
        [f32(rows, width) for _ in targets],
        [IN_VMEM] * 3,
        cost=kernel_cost(rows, count, width),
    )(codes, lookup_grads, after)


def finish_first_ring(token, own0, back0, next0, own1, next1, back1):
    rows, width = own0.shape
    slots = rows // SIDE

    def body(token_ref, o0, b0, n0, o1, n1, b1, *out_refs):
        for offset in range(SIDE):
            piece = pl.ds(offset * slots, slots)
            for table, refs in enumerate([(o0, b0, n0), (o1, n1, b1)]):
                total = refs[0][piece, :] + refs[1][piece, :] + refs[2][piece, :]
                out_refs[offset][pl.ds(table * slots, slots), :] = total

    return call(body, "finish_first_ring", [f32(2 * slots, width)] * SIDE, [IN_VMEM] * 7)(
        token, own0, back0, next0, own1, next1, back1
    )


def finish_second_ring(unique_rows, pieces):
    rows, width = pieces[0].shape
    slots = rows // 2
    chips = SIDE
    bucket = slots // (CORES * chips)
    height = 2 * bucket + 8

    def body(unique_ref, p0, p1, p2, p3, kept, given):
        group = position()[0]
        core = group & (CORES - 1)
        numbers = unique_ref[...].astype(jnp.float32) + 1.0
        for offset in range(chips):
            chip = (lax.shift_right_logical(group, 1) + offset) & (chips - 1)
            for out_ref, owner in [(kept, core), (given, 1 - core)]:
                for table in range(2):
                    start = table * slots + (chip * CORES + owner) * bucket
                    piece = pl.ds(pl.multiple_of(start, bucket), bucket)
                    total = (p0[piece, :] + p1[piece, :]) + (p2[piece, :] + p3[piece, :])
                    out_ref[offset, pl.ds(table * bucket, bucket), :] = total
                out_ref[offset, pl.ds(2 * bucket, 8), :] = jnp.zeros((8, width), jnp.float32)
                out_ref[offset, pl.ds(2 * bucket, 2), pl.ds(0, LANES)] = numbers

    return call(
        body, "finish_second_ring", [f32(chips, height, width)] * 2, [IN_VMEM] * (1 + SIDE)
    )(unique_rows, *pieces)


def eye():
    shape = (LANES, LANES)
    return lax.broadcasted_iota(jnp.int32, shape, 0) == lax.broadcasted_iota(jnp.int32, shape, 1)


def turn(vector, diagonal):
    axis = 1 if vector.shape[0] == 1 else 0
    square = jnp.where(diagonal, jnp.broadcast_to(vector, (LANES, LANES)), 0.0)
    return jnp.sum(square, axis=axis, keepdims=True)


def apply_update(arrived, tables, accums):
    rows_dev, width = tables.shape[1:]
    rows = 256
    count = rows_dev // rows
    height = arrived[0].shape[0] // CORES
    bucket = (height - 8) // 2

    def body(*refs):
        arrived_refs = refs[:SIDE]
        tables_ref, accums_ref, new_tables_hbm, new_accums_ref, done_ref, sems = refs[SIDE:]
        diagonal = eye()
        copies = []
        sources = [(ref, core * height) for ref in arrived_refs for core in range(CORES)]
        group = position()[0]
        lane = lax.broadcasted_iota(jnp.int32, (8, LANES), 1) // bucket
        local_rows = jnp.zeros((8, LANES), jnp.int32)
        for spot, (ref, first) in enumerate(sources):
            listed = ref[pl.ds(first + 2 * bucket, 8), pl.ds(0, LANES)].astype(jnp.int32)
            listed = pltpu.roll(listed, ((spot - group) * bucket) & (LANES - 1), 1)
            local_rows = jnp.where(lane == spot, listed, local_rows)
        local_rows = jnp.where(local_rows == 0, -1, (local_rows - 1) & (rows_dev - 1))
        for table in range(2):
            values = jnp.concatenate(
                [ref[pl.ds(first + table * bucket, bucket), :] for ref, first in sources]
            )
            high = values.astype(jnp.bfloat16)
            rest = values - high.astype(jnp.float32)
            middle = rest.astype(jnp.bfloat16)
            low = (rest - middle.astype(jnp.float32)).astype(jnp.bfloat16)
            pieces = jnp.concatenate([high, middle, low], axis=0)
            for block in range(count):
                base = block * rows
                hit = lax.broadcasted_iota(jnp.int32, (rows, LANES), 0) + base == local_rows[table : table + 1]
                onehot = jnp.where(hit, jnp.float32(1), jnp.float32(0)).astype(jnp.bfloat16)
                onehot = jnp.concatenate([onehot] * 3, axis=1)
                row_grads = jnp.dot(onehot, pieces, preferred_element_type=jnp.float32)
                squares = jnp.sum(row_grads * row_grads, axis=1, keepdims=True)
                for start in range(0, rows, LANES):
                    place = pl.ds(base + start, LANES)
                    square = turn(squares[start : start + LANES], diagonal)
                    accum = accums_ref[table : table + 1, place] + square * (1.0 / width)
                    new_accums_ref[table : table + 1, place] = accum
                    scale = turn(learning_rate / (jnp.sqrt(accum) + epsilon), diagonal)
                    step = row_grads[start : start + LANES] * scale
                    done_ref[table, place, :] = tables_ref[table, place, :] - step
                place = pl.ds(base, rows)
                copies.append(
                    pltpu.make_async_copy(
                        done_ref.at[table, place],
                        new_tables_hbm.at[table, place],
                        sems.at[table * count + block],
                    )
                )
                copies[-1].start()
        for copy in copies:
            copy.wait()

    return call(
        body,
        "apply_update",
        [f32(*tables.shape), f32(*accums.shape)],
        [IN_VMEM] * (SIDE + 2),
        [IN_HBM, IN_VMEM],
        [pltpu.VMEM(tables.shape, jnp.float32), pltpu.SemaphoreType.DMA((2 * count,))],
    )(*arrived, tables, accums)


def local(lookup_grads, slot_index, unique_rows, tables, accums):
    n_group = lax.axis_size("group")
    n_local = lax.axis_size("local")

    def send(value, step, ring=0):
        return lax.ppermute(value, AXES, ring_pairs(n_group, n_local, ring, step))

    def send_along(value, step):
        return lax.ppermute(
            value, "group", [(i, (i + CORES * step) % n_group) for i in range(n_group)]
        )

    far0, far1, grads, codes = first_sums(slot_index, lookup_grads, [(0, 2), (1, 2)])
    back0, next1 = slot_sums(codes, grads, [(0, 3), (1, 1)], far0)
    next0, back1 = slot_sums(codes, grads, [(0, 1), (1, 3)], next1)
    own0, own1 = slot_sums(codes, grads, [(0, 0), (1, 0)], back1)
    far0 = send(far0, 1)
    far1 = send(far1, -1)
    next1 = send(next1, 1)
    back0 = send(back0, -1)
    next0 = send(next0 + far0, 1)
    back1 = send(back1 + far1, -1)

    token = lax.ppermute(
        sum(value[:8, :LANES] for value in (next0, back0, next1, back1, own0)),
        "group",
        [(i, i ^ 1) for i in range(n_group)],
    )

    pieces = finish_first_ring(token, own0, back0, next0, own1, next1, back1)
    pieces = [pieces[0]] + [send(pieces[step], step, ring=1) for step in (2, 1, 3)]
    kept, given = finish_second_ring(unique_rows, pieces)

    swapped = lax.ppermute(given, "group", [(i, i ^ 1) for i in range(n_group)])
    arrived = [jnp.concatenate([kept[step], swapped[step]]) for step in range(SIDE)]
    arrived = [arrived[0]] + [send_along(arrived[step], step) for step in (2, 1, 3)]
    new_tables, new_accums = apply_update(arrived, tables, accums)
    return (new_tables, new_accums)


def solution(mesh):
    return jax.shard_map(
        local,
        mesh=mesh,
        in_specs=(
            P(("group", "local"), None),
            P(None, ("group", "local")),
            P(None, ("group", "local")),
            P(None, ("group", "local"), None),
            P(None, ("group", "local")),
        ),
        out_specs=(P(None, ("group", "local"), None), P(None, ("group", "local"))),
        check_vma=False,
    )
```
